32 devices in a mesh: fsdp: 4 (over z), ctx: 2 (over x), tp: 4 (over y, core).
Axes of the slice: x: 2, y: 2, z: 4, core: 2. Of those that a mesh axis runs over, the one named last changes fastest.
Arguments:
- tokens: bfloat16 [12288, 2048], P(('fsdp', 'ctx'), 'tp'), may hold values from -6 to 6
- cotangent: bfloat16 [12288, 2048], P(('fsdp', 'ctx'), 'tp'), may hold values from -6 to 6
- lengths: int32 [4, 6], replicated, may hold values from 1 to 1024, 3072 in all within a row
- order: int32 [24], replicated, may hold values from 0 to 23, each once
- w_query: bfloat16 [2048, 2048], P('fsdp', 'tp'), may hold values from -0.1875 to 0.1875
- w_key: bfloat16 [2048, 2048], P('fsdp', 'tp'), may hold values from -0.1875 to 0.1875
- w_value: bfloat16 [2048, 2048], P('fsdp', 'tp'), may hold values from -0.125 to 0.125
- w_output: bfloat16 [2048, 2048], P('fsdp', 'tp'), may hold values from -0.375 to 0.375
- w_gate: bfloat16 [2048, 8192], P('fsdp', 'tp'), may hold values from -0.125 to 0.125
- w_up: bfloat16 [2048, 8192], P('fsdp', 'tp'), may hold values from -0.125 to 0.125
- w_down: bfloat16 [2048, 8192], P('fsdp', 'tp'), may hold values from -0.0625 to 0.0625
Outputs:
- layer_out: bfloat16 [12288, 2048], P(('fsdp', 'ctx'), 'tp')
- input_grad: bfloat16 [12288, 2048], P(('fsdp', 'ctx'), 'tp')
- grad_query: float32 [2048, 2048], P('fsdp', 'tp')
- grad_key: float32 [2048, 2048], P('fsdp', 'tp')
- grad_value: float32 [2048, 2048], P('fsdp', 'tp')
- grad_output: float32 [2048, 2048], P('fsdp', 'tp')
- grad_gate: float32 [2048, 8192], P('fsdp', 'tp')
- grad_up: float32 [2048, 8192], P('fsdp', 'tp')
- grad_down: float32 [2048, 8192], P('fsdp', 'tp')
The draws below stay inside these ranges and needn't reach their ends.
Inputs may be any that keep to these rules, and one draw needn't show every extreme that they name: Each row gives the lengths of the 6 sequences dealt to one index of fsdp; a row sums to the tokens of that index (1536 times the size of ctx), and its longest sequence has exactly 1024 tokens. `order`: A permutation of the sequence numbers.
All inputs are finite; a program needn't handle non-finite values.
Results may differ from the reference program's by a relative error of at most 0.019.
Values may be sent and summed in bfloat16 or wider, within the bound.
No kernel may reach another device: no remote copies, remote signals or barrier semaphores. Data moves between devices by JAX's collectives and lax.ppermute only.
A program may use at most 320 MiB of HBM per device.

```python
import math
import jax
import jax.numpy as jnp
import numpy as np
from jax import lax

D = 2048
H = 16
HD = 128
FF = 8192
TOK_DEV = 1536
MAXLEN = 1024
SEQ_GRP = 6
NSEQ = 24
TOKENS = 12288
N_FSDP = 4
N_CTX = 2


def block_scale(own_key, extent, cuts, low, largest):
    loudness = 1.0
    for axis_at, parts in cuts:
        steps = jax.random.uniform(jax.random.fold_in(jax.random.fold_in(own_key, 6), axis_at), (parts,), jnp.float32, low / len(cuts), largest / len(cuts))
        loudness = loudness * jnp.repeat(jnp.exp(steps), extent[axis_at] // parts).reshape((-1,) + (1,) * (len(extent) - 1 - axis_at))
    return loudness


def profile(number_of, total, most, skew):
    loads = [(1 << 20) // math.isqrt(grade ** skew) + 1 for grade in range(2, number_of + 1)]
    surplus, given = total - most - (number_of - 1), [1] * (number_of - 1)
    while surplus > 0:
        movable = [i for i in range(number_of - 1) if given[i] < most]
        whole, budget = sum([loads[i] for i in movable]), surplus
        for i in movable:
            extra = min(most - given[i], max(1, budget * loads[i] // whole), surplus)
            given[i] = given[i] + extra
            surplus = surplus - extra
    return np.array([most] + given)


def ragged(stream_key, number_of, total, most, slope):
    if number_of == 2:
        one = jax.random.randint(stream_key, (), max(1, total - most), min(most, total - 1) + 1)
        return jnp.stack([one, total - one])
    tallies = jnp.asarray(profile(number_of, total, most, slope), jnp.int32)
    couples = (number_of - 1) // 2
    source_of, taker = tallies[1:1 + 2 * couples:2], tallies[2:2 + 2 * couples:2]
    room = jnp.minimum(source_of - 1, most - taker)
    shifted = jax.random.randint(jax.random.fold_in(stream_key, 1), (couples,), 0, 1 << 20) % (room + 1)
    tallies = tallies.at[1:1 + 2 * couples:2].set(source_of - shifted).at[2:2 + 2 * couples:2].set(taker + shifted)
    return tallies[jax.random.permutation(jax.random.fold_in(stream_key, 2), number_of)]


def gaussian(own_key, dims, deviation, most, shards=(), kind=jnp.bfloat16):
    level = block_scale(own_key, dims, shards, -0.22, 0.18) if shards else 1.0
    values = jax.random.normal(own_key, dims, jnp.float32) * deviation * level
    return jnp.minimum(jnp.maximum(values, -most), most).astype(kind)


def setup_inputs(seed: int = 0) -> dict:
    key_of = jax.random.split(jax.random.key(seed), 12)
    tokens = gaussian(key_of[0], (TOKENS, D), 1.0, 6.0, ((0, 8), (1, 4)))
    cotangent = gaussian(key_of[1], (TOKENS, D), 1.0, 6.0, ((0, 8), (1, 4)))
    lengths = jax.vmap(lambda own: ragged(own, SEQ_GRP, N_CTX * TOK_DEV, MAXLEN, 2))(jax.random.split(key_of[2], N_FSDP)).reshape((N_FSDP, SEQ_GRP)).astype(jnp.int32)
    order = jax.random.permutation(key_of[3], NSEQ).astype(jnp.int32)
    w_query = gaussian(key_of[4], (D, D), (D // 2) ** -0.5, 0.1875, ((0, 4), (1, 4)))
    w_key = gaussian(key_of[5], (D, D), (D // 2) ** -0.5, 0.1875, ((0, 4), (1, 4)))
    w_value = gaussian(key_of[6], (D, D), D ** -0.5, 0.125, ((0, 4), (1, 4)))
    w_output = gaussian(key_of[7], (D, D), (D // 8) ** -0.5, 0.375, ((0, 4), (1, 4)))
    w_gate = gaussian(key_of[8], (D, FF), D ** -0.5, 0.125, ((0, 4), (1, 4)))
    w_up = gaussian(key_of[9], (D, FF), D ** -0.5, 0.125, ((0, 4), (1, 4)))
    w_down = gaussian(key_of[10], (D, FF), FF ** -0.5, 0.0625, ((0, 4), (1, 4)))
    return {"tokens": tokens, "cotangent": cotangent, "lengths": lengths, "order": order, "w_query": w_query, "w_key": w_key, "w_value": w_value, "w_output": w_output, "w_gate": w_gate, "w_up": w_up, "w_down": w_down}


@jax.custom_vjp
def low(v):
    return lax.optimization_barrier(v.astype(jnp.bfloat16)).astype(jnp.float32)

@jax.custom_vjp
def low_back(v):
    return v

def low_keep(v):
    return (low(v), None)

def low_pass(kept, grad):
    return (grad,)

def back_keep(v):
    return (v, None)

def back_low(kept, grad):
    return (low(grad),)
low.defvjp(low_keep, low_pass)
low_back.defvjp(back_keep, back_low)
PRECISE = lax.Precision.HIGHEST
EPSILON = 1e-05
NEG_FILL = -1e+30

def matmul(left, right):
    return jnp.dot(left, right, precision=PRECISE, preferred_element_type=jnp.float32)

def normalize(values):
    average = lax.optimization_barrier(jnp.mean(values, axis=-1, keepdims=True))
    centred = values - average
    spread = lax.optimization_barrier(jnp.mean(centred * centred, axis=-1, keepdims=True))
    return centred * lax.rsqrt(spread + EPSILON)

def rope_tables(within):
    half_size = HD // 2
    steps_idx = jnp.arange(half_size, dtype=jnp.float32)
    freq = jnp.exp(steps_idx * (-2.0 * math.log(10000.0) / HD))
    angle = within.astype(jnp.float32)[:, None] * freq[None, :]
    angle = jnp.concatenate([angle, angle], axis=1)
    return (jnp.cos(angle)[:, None, :], jnp.sin(angle)[:, None, :])

def rotate(vector, cos_tab, sin_tab):
    half_size = vector.shape[-1] // 2
    turned = jnp.concatenate([-vector[..., half_size:], vector[..., :half_size]], axis=-1)
    return vector * cos_tab + turned * sin_tab

def positions(lengths, order):
    seq_len = lengths.reshape(-1).astype(jnp.int32)
    dealt_start = (jnp.cumsum(seq_len) - seq_len).astype(jnp.int32)
    order_len = seq_len[order]
    slot_start = (jnp.cumsum(order_len) - order_len).astype(jnp.int32)
    orig_start = jnp.zeros(seq_len.shape, jnp.int32).at[order].set(slot_start)
    index = jnp.arange(TOKENS, dtype=jnp.int32)
    inside = (index[:, None] >= dealt_start[None, :]).astype(jnp.int32)
    seq_id = (lax.optimization_barrier(jnp.sum(inside, axis=1)) - 1).astype(jnp.int32)
    within = (index - dealt_start[seq_id]).astype(jnp.int32)
    source = (orig_start[seq_id] + within).astype(jnp.int32)
    return (seq_id, within, source)

def attend_group(group):
    query, keyed, valued, seq_id, within = group
    scores = jnp.einsum('qhd,khd->hqk', query, keyed, precision=PRECISE) * HD ** (-0.5)
    scores = low_back(scores)
    allowed = (seq_id[:, None] == seq_id[None, :]) & (within[None, :] <= within[:, None])
    probs = jax.nn.softmax(jnp.where(allowed[None], scores, NEG_FILL), axis=-1)
    return jnp.einsum('hqk,khd->qhd', low(probs), valued, precision=PRECISE)

def reference(tokens, cotangent, lengths, order, w_query, w_key, w_value, w_output, w_gate, w_up, w_down):
    seq_id, within, source = positions(lengths, order)
    inverse = jnp.zeros((TOKENS,), jnp.int32).at[source].set(jnp.arange(TOKENS, dtype=jnp.int32))
    dealt_x = tokens.astype(jnp.float32)[source]
    dealt_g = cotangent.astype(jnp.float32)[source]
    cos_tab, sin_tab = rope_tables(within)
    group_rows = N_CTX * TOK_DEV

    def group_view(array):
        return array.reshape((N_FSDP, group_rows) + array.shape[1:])

    def forward(resid, m_query, m_key, m_value, m_output, m_gate, m_up, m_down):
        hidden1 = low(normalize(resid))
        query = low(rotate(low_back(matmul(hidden1, m_query)).reshape(TOKENS, H, HD), cos_tab, sin_tab))
        keyed = low(rotate(low_back(matmul(hidden1, m_key)).reshape(TOKENS, H, HD), cos_tab, sin_tab))
        valued = low_back(low(matmul(hidden1, m_value))).reshape(TOKENS, H, HD)
        attended = lax.map(jax.checkpoint(attend_group), (group_view(query), group_view(keyed), group_view(valued), group_view(seq_id), group_view(within)))
        mixed = low_back(low(attended.reshape(TOKENS, D)))
        branch = low_back(matmul(mixed, m_output.T))
        resid1 = resid + branch
        hidden2 = low(normalize(resid1))
        gate_proj = low_back(matmul(hidden2, m_gate))
        up_proj = low_back(matmul(hidden2, m_up))
        active = low_back(low(jax.nn.silu(gate_proj) * up_proj))
        return resid1 + matmul(active, m_down.T)
    weights = (w_query.astype(jnp.float32), w_key.astype(jnp.float32), w_value.astype(jnp.float32), w_output.astype(jnp.float32), w_gate.astype(jnp.float32), w_up.astype(jnp.float32), w_down.astype(jnp.float32))
    result, pull = jax.vjp(forward, dealt_x, *weights)
    grads = pull(dealt_g)
    layer_out = result[inverse].astype(jnp.bfloat16)
    input_grad = grads[0][inverse].astype(jnp.bfloat16)
    return (layer_out, input_grad, grads[1], grads[2], grads[3], grads[4], grads[5], grads[6], grads[7])
```

```python
import functools
import math

import jax
import jax.numpy as jnp
from jax import lax
from jax.experimental import pallas as pl
from jax.experimental.pallas import tpu as pltpu
from jax.sharding import PartitionSpec as P

HD = 128
HALO = 1024
EPSILON = 1e-05
NEG_FILL = -1e30
PLANE = ("ctx", "tp")
BF = jnp.bfloat16
F32 = jnp.float32


def dot_plain(left, right):
    return jnp.dot(left, right, preferred_element_type=F32)


def dot_last(left, right):
    return lax.dot_general(left, right, (((1,), (1,)), ((), ())), preferred_element_type=F32)


def dot_rows(left, right):
    return lax.dot_general(left, right, (((0,), (0,)), ((), ())), preferred_element_type=F32)


def normalize(values):
    average = jnp.mean(values, axis=-1, keepdims=True)
    centred = values - average
    spread = jnp.mean(centred * centred, axis=-1, keepdims=True)
    inv_dev = lax.rsqrt(spread + EPSILON)
    return (centred * inv_dev, inv_dev)


def norm_back(grad, normed, inv_dev):
    grad_mean = jnp.mean(grad, axis=-1, keepdims=True)
    cross_mean = jnp.mean(grad * normed, axis=-1, keepdims=True)
    return inv_dev * (grad - grad_mean - normed * cross_mean)


def slots(lengths, order):
    seq_len = lengths.reshape(-1)
    seq_ids = jnp.arange(seq_len.shape[0], dtype=jnp.int32)
    picks = order[:, None] == seq_ids[None, :]
    order_len = jnp.sum(jnp.where(picks, seq_len[None, :], 0), axis=1)
    return jnp.cumsum(order_len) - order_len


def first_of(index, starts):
    inside = index[:, None] >= starts[None, :]
    return jnp.max(jnp.where(inside, starts[None, :], 0), axis=1)


def qkv_kernel(heads, x_ref, own_ref, oth_ref, cos_ref, sin_ref, h_ref, q_ref, k_ref, v_ref, e_ref):
    values = x_ref[...].astype(F32)
    normed, _ = normalize(values)
    hidden = normed.astype(BF)
    h_ref[...] = hidden
    cos, sin = cos_ref[...], sin_ref[...]
    width = heads * HD
    for piece, w_ref in enumerate((own_ref, oth_ref)):
        out = dot_plain(hidden, w_ref[...])
        for head in range(heads):
            to = (piece * heads + head) * HD
            swapped = ((1 - piece) * heads + head) * HD
            query = out[:, head * HD : (head + 1) * HD]
            key = out[:, width + head * HD : width + (head + 1) * HD]
            value = out[:, 2 * width + head * HD : 2 * width + (head + 1) * HD].astype(BF)
            query = (query * cos + pltpu.roll(query, HD // 2, 1) * sin).astype(BF)
            key = (key * cos + pltpu.roll(key, HD // 2, 1) * sin).astype(BF)
            q_ref[:, to : to + HD] = query
            k_ref[:, to : to + HD] = key
            v_ref[:, to : to + HD] = value
            e_ref[:, swapped : swapped + HD] = key
            e_ref[:, 2 * width + swapped : 2 * width + swapped + HD] = value


def project(x, w_own, w_oth, cos_tab, sin_tab, heads):
    rows, width = x.shape
    block = rows // 3
    skip = rows // block - HALO // block
    local = 2 * heads * HD
    row = lambda i: (i, 0)
    return pl.pallas_call(
        functools.partial(qkv_kernel, heads),
        grid=(rows // block,),
        in_specs=[
            pl.BlockSpec((block, width), row),
            pl.BlockSpec((width, 3 * heads * HD), lambda i: (0, 0)),
            pl.BlockSpec((width, 3 * heads * HD), lambda i: (0, 0)),
            pl.BlockSpec((block, HD), lambda i: (i + HALO // block, 0)),
            pl.BlockSpec((block, HD), lambda i: (i + HALO // block, 0)),
        ],
        out_specs=[
            pl.BlockSpec((block, width), row),
            pl.BlockSpec((block, local), row),
            pl.BlockSpec((block, local), row),
            pl.BlockSpec((block, local), row),
            pl.BlockSpec((block, 2 * local), lambda i: (jnp.maximum(i - skip, 0), 0)),
        ],
        out_shape=[
            jax.ShapeDtypeStruct((rows, width), BF),
            jax.ShapeDtypeStruct((rows, local), BF),
            jax.ShapeDtypeStruct((rows, local), BF),
            jax.ShapeDtypeStruct((rows, local), BF),
            jax.ShapeDtypeStruct((HALO, 2 * local), BF),
        ],
        cost_estimate=pl.CostEstimate(
            flops=2 * rows * width * 3 * local, bytes_accessed=20_000_000, transcendentals=0
        ),
        name="norm_project",
    )(x, w_own, w_oth, cos_tab, sin_tab)


def allowed_keys(first_ref, step, block):
    span = block + HALO
    keys = lax.broadcasted_iota(jnp.int32, (block, span), 1)
    rows = lax.broadcasted_iota(jnp.int32, (block, span), 0)
    first = first_ref[...] - step * block
    return (keys >= first) & (keys <= rows + HALO)


def attend_kernel(q_ref, k_ref, v_ref, ke_ref, ve_ref, first_ref, o_ref, lse_ref, keys, values):
    step = pl.program_id(1)
    block = q_ref.shape[0]

    @pl.when(step == 0)
    def _():
        keys[:HALO] = ke_ref[...]
        keys[HALO:] = k_ref[...]
        values[:HALO] = ve_ref[...]
        values[HALO:] = v_ref[...]

    window = pl.ds(pl.multiple_of(step * block, block), block + HALO)
    raw = dot_last(q_ref[...], keys[window, :]) * (HD**-0.5)
    raw = jnp.where(allowed_keys(first_ref, step, block), raw, NEG_FILL)
    top = jnp.max(raw, axis=-1, keepdims=True)
    expo = jnp.exp(raw - top)
    denom = jnp.sum(expo, axis=-1, keepdims=True)
    probs = (expo * (1.0 / denom)).astype(BF)
    o_ref[...] = dot_plain(probs, values[window, :]).astype(BF)
    lse_ref[...] = top + jnp.log(denom)


def attend(q, k, v, halo, first, block=256):
    rows, local = q.shape
    heads = local // HD
    span = block + HALO
    return pl.pallas_call(
        attend_kernel,
        grid=(heads, rows // block),
        in_specs=[
            pl.BlockSpec((block, HD), lambda h, i: (i, h)),
            pl.BlockSpec((rows, HD), lambda h, i: (0, h)),
            pl.BlockSpec((rows, HD), lambda h, i: (0, h)),
            pl.BlockSpec((HALO, HD), lambda h, i: (0, h)),
            pl.BlockSpec((HALO, HD), lambda h, i: (0, h + heads)),
            pl.BlockSpec((block, 1), lambda h, i: (i, 0)),
        ],
        out_specs=[
            pl.BlockSpec((block, HD), lambda h, i: (i, h)),
            pl.BlockSpec((None, block, 1), lambda h, i: (h, i, 0)),
        ],
        out_shape=[
            jax.ShapeDtypeStruct((rows, local), BF),
            jax.ShapeDtypeStruct((heads, rows, 1), F32),
        ],
        scratch_shapes=[pltpu.VMEM((HALO + rows, HD), BF)] * 2,
        cost_estimate=pl.CostEstimate(
            flops=8 * rows * span * HD * heads,
            bytes_accessed=10_000_000,
            transcendentals=rows * span * heads,
        ),
        name="attend",
    )(q, k, v, halo, halo, first)


def rotate_back(grad, cos, sin):
    return grad * cos - pltpu.roll(grad, HD // 2, 1) * sin


def attend_back_kernel(
    q_ref, k_ref, v_ref, ke_ref, ve_ref, first_ref, lse_ref, do_ref, cos_ref, sin_ref,
    dq_ref, dk_ref, dv_ref, dke_ref, dve_ref, keys, values, dkeys, dvalues,
):
    step = pl.program_id(1)
    block = q_ref.shape[0]
    scale = HD**-0.5

    @pl.when(step == 0)
    def _():
        keys[:HALO] = ke_ref[...]
        keys[HALO:] = k_ref[...]
        values[:HALO] = ve_ref[...]
        values[HALO:] = v_ref[...]
        dkeys[...] = jnp.zeros_like(dkeys)
        dvalues[...] = jnp.zeros_like(dvalues)

    window = pl.ds(pl.multiple_of(step * block, block), block + HALO)
    query, dout = q_ref[...], do_ref[...]
    raw = dot_last(query, keys[window, :]) * scale
    probs = jnp.where(allowed_keys(first_ref, step, block), jnp.exp(raw - lse_ref[...]), 0.0)
    dprob = dot_last(dout, values[window, :])
    delta = jnp.sum(probs * dprob, axis=-1, keepdims=True)
    dscore = (probs * (dprob - delta)).astype(BF)
    mine = pl.ds(pl.multiple_of(HALO + step * block, block), block)
    dquery = dot_plain(dscore, keys[window, :]) * scale
    dq_ref[...] = rotate_back(dquery, cos_ref[mine, :], sin_ref[mine, :]).astype(BF)
    dkeys[window, :] += dot_rows(dscore, query)
    dvalues[window, :] += dot_rows(probs.astype(BF), dout)

    @pl.when(step == pl.num_programs(1) - 1)
    def _():
        dkey = rotate_back(dkeys[...] * scale, cos_ref[...], sin_ref[...])
        dke_ref[...] = dkey[:HALO].astype(BF)
        dk_ref[...] = dkey[HALO:]
        dve_ref[...] = dvalues[:HALO].astype(BF)
        dv_ref[...] = dvalues[HALO:]


def attend_back(q, k, v, halo, first, lse, dout, cos_tab, sin_tab, block=256):
    rows, local = q.shape
    heads = local // HD
    span = block + HALO
    column = pl.BlockSpec((rows, HD), lambda h, i: (0, h))
    piece = pl.BlockSpec((block, HD), lambda h, i: (i, h))
    table = pl.BlockSpec((HALO + rows, HD), lambda h, i: (0, 0))
    edge = pl.BlockSpec((HALO, HD), lambda h, i: (0, h))
    return pl.pallas_call(
        attend_back_kernel,
        grid=(heads, rows // block),
        in_specs=[
            piece,
            column,
            column,
            edge,
            pl.BlockSpec((HALO, HD), lambda h, i: (0, h + heads)),
            pl.BlockSpec((block, 1), lambda h, i: (i, 0)),
            pl.BlockSpec((None, block, 1), lambda h, i: (h, i, 0)),
            piece,
            table,
            table,
        ],
        out_specs=[piece, column, column, edge, edge],
        out_shape=[
            jax.ShapeDtypeStruct((rows, local), BF),
            jax.ShapeDtypeStruct((rows, local), F32),
            jax.ShapeDtypeStruct((rows, local), F32),
            jax.ShapeDtypeStruct((HALO, local), BF),
            jax.ShapeDtypeStruct((HALO, local), BF),
        ],
        scratch_shapes=[pltpu.VMEM((HALO + rows, HD), BF)] * 2
        + [pltpu.VMEM((HALO + rows, HD), F32)] * 2,
        cost_estimate=pl.CostEstimate(
            flops=20 * rows * span * HD * heads,
            bytes_accessed=20_000_000,
            transcendentals=rows * span * heads,
        ),
        name="attend_back",
    )(q, k, v, halo, halo, first, lse, dout, cos_tab, sin_tab)


class Plane:
    def __init__(self):
        self.nc, self.nt = lax.axis_size("ctx"), lax.axis_size("tp")
        assert self.nc == 2 and self.nt % 2 == 0
        self.hi = self.nt // self.nc
        self.ranks = self.nc * self.hi
        tp_place = lax.axis_index("tp")
        self.c = lax.axis_index("ctx")
        self.h, self.k = tp_place // self.nc, tp_place % self.nc
        self.r = self.c * self.hi + self.h

    def perm(self, move):
        pairs = []
        for c in range(self.nc):
            for h in range(self.hi):
                for k in range(self.nc):
                    c2, h2, k2 = move(c, h, k)
                    pairs.append((c * self.nt + h * self.nc + k, c2 * self.nt + h2 * self.nc + k2))
        return pairs

    def spread_rows(self, block):
        full = jnp.zeros((block.shape[0], block.shape[1] * self.nt), block.dtype)
        for jh in range(self.hi):
            for jk in range(self.nc):
                move = lambda c, h, k: (k ^ jk, h ^ jh, c)
                got = lax.ppermute(block, PLANE, self.perm(move))
                place = (self.h ^ jh) * self.nc + (self.c ^ jk)
                full = lax.dynamic_update_slice(full, got, (0, place * block.shape[1]))
        return full

    def to_blocks(self, mine):
        chunk, width = mine.shape
        cols = width // self.nt
        full = jnp.zeros((chunk * self.ranks, cols), mine.dtype)
        for jh in range(self.hi):
            for jk in range(self.nc):
                move = lambda c, h, k: (k, h ^ jh, c ^ jk)
                place = (self.h ^ jh) * self.nc + (self.c ^ jk)
                piece = lax.dynamic_slice_in_dim(mine, place * cols, cols, 1)
                got = lax.ppermute(piece, PLANE, self.perm(move))
                rank = (self.k ^ jk) * self.hi + (self.h ^ jh)
                full = lax.dynamic_update_slice(full, got, (rank * chunk, 0))
        return full

    def swap(self, value, j):
        def move(c, h, k):
            rank = (c * self.hi + h) ^ j
            return rank // self.hi, rank % self.hi, k

        return lax.ppermute(value, PLANE, self.perm(move))

    def chunk_of(self, value, j):
        size = value.shape[0] // self.ranks
        return lax.dynamic_slice_in_dim(value, (self.r ^ j) * size, size, 0)

    def turn(self, value):
        return jnp.concatenate([self.chunk_of(value, j) for j in range(self.ranks)], axis=0)

    def gather(self, mine):
        return jnp.concatenate([mine] + [self.swap(mine, j) for j in range(1, self.ranks)], axis=0)

    def pair(self, value):
        perm = [(t, t ^ 1) for t in range(self.nt)]
        return lax.ppermute(value, "tp", perm)


def body(
    tokens, cotangent, lengths, order, w_query, w_key, w_value, w_output, w_gate, w_up, w_down
):
    plane = Plane()
    rows = tokens.shape[0]
    nf, nc, nt, ranks = lax.axis_size("fsdp"), plane.nc, plane.nt, plane.ranks
    z = lax.axis_index("fsdp")
    chunk = rows // ranks
    head_cols = w_query.shape[1] // nc
    heads = head_cols // HD

    def part(weight):
        size = weight.shape[1] // nc
        return lax.dynamic_slice_in_dim(weight, plane.c * size, size, 1)

    def collect(shard):
        own = lax.all_gather(shard, "fsdp", axis=0, tiled=True)
        return own, plane.pair(own)

    attn_own, attn_oth = collect(
        jnp.concatenate([part(w) for w in (w_query, w_key, w_value, w_output)], axis=1)
    )
    wg = collect(part(w_gate))
    wu = collect(part(w_up))
    wd = collect(part(w_down))

    full_x = plane.spread_rows(tokens)
    full_g = plane.spread_rows(cotangent)
    base = (z * nc + plane.k) * rows - HALO
    index = base + jnp.arange(HALO + rows, dtype=jnp.int32)
    starts = first_of(index, slots(lengths, order))
    within = index - starts
    first = (starts[HALO:] - base)[:, None]
    lane = jnp.arange(HD, dtype=jnp.int32)
    freq = jnp.exp((lane % (HD // 2)).astype(F32) * (-2.0 * math.log(10000.0) / HD))
    angle = within.astype(F32)[:, None] * freq[None, :]
    cos_tab = jnp.cos(angle)
    sin_tab = jnp.sin(angle) * jnp.where(lane < HD // 2, -1.0, 1.0)[None, :]

    hidden1, query, key, value, edge = project(full_x, attn_own, attn_oth, cos_tab, sin_tab, heads)
    onward = []
    for f in range(nf):
        for h in range(plane.hi):
            for k in range(nc):
                to = f * nc + k + 1
                if to < nf * nc:
                    onward.append((f * nt + h * nc + k, to // nc * nt + h * nc + to % nc))
    backward = [(b, a) for a, b in onward]
    halo = lax.ppermute(edge, ("fsdp", "tp"), onward)
    mixed, lse = attend(query, key, value, halo, first)

    wo = jnp.concatenate([attn_own[:, 3 * head_cols :], attn_oth[:, 3 * head_cols :]], axis=1)
    resid = plane.chunk_of(full_x, 0).astype(F32)
    resid1 = resid + dot_last(plane.chunk_of(mixed, 0), wo)
    for j in range(1, ranks):
        resid1 = resid1 + plane.swap(
            dot_last(plane.chunk_of(mixed, j), wo).astype(BF), j
        ).astype(F32)
    normed2, inv_dev2 = normalize(resid1)
    hidden2 = plane.gather(normed2.astype(BF))

    grad_rows = plane.turn(full_g)
    acts, dgates, dups = [], [], []
    for piece in range(2):
        dact = dot_plain(grad_rows, wd[piece]).astype(BF).astype(F32)
        gate = dot_plain(hidden2, wg[piece])
        up = dot_plain(hidden2, wu[piece])
        sig = jax.nn.sigmoid(gate)
        silu = gate * sig
        acts.append((silu * up).astype(BF))
        dgates.append((dact * up * sig * (1.0 + gate * (1.0 - sig))).astype(BF))
        dups.append((dact * silu).astype(BF))

    def scatter(parts):
        total = parts[:chunk]
        low = parts.astype(BF)
        for j in range(1, ranks):
            total = total + plane.swap(low[j * chunk : (j + 1) * chunk], j).astype(F32)
        return total

    dh2 = (
        dot_last(dgates[0], wg[0])
        + dot_last(dups[0], wu[0])
        + dot_last(dgates[1], wg[1])
        + dot_last(dups[1], wu[1])
    )
    dx1 = grad_rows[:chunk].astype(F32) + norm_back(scatter(dh2), normed2, inv_dev2)
    da = plane.gather(dx1.astype(BF))
    mlp = dot_last(acts[0], wd[0]) + dot_last(acts[1], wd[1])
    layer_out = plane.to_blocks((resid1 + scatter(mlp)).astype(BF))

    def share(left, right_own, right_oth, cut=None):
        other = plane.pair(dot_rows(left, right_oth).astype(BF))
        total = (dot_rows(left, right_own) + other.astype(F32)).astype(BF)
        return lax.psum_scatter(total, "fsdp", scatter_dimension=0, tiled=True)

    def finish(mine):
        perm = [(0, 1), (1, 0)]
        other = lax.ppermute(mine, "ctx", perm)
        here = plane.c == 0
        return jnp.concatenate(
            [jnp.where(here, mine, other), jnp.where(here, other, mine)], axis=1
        ).astype(F32)

    grad_down = finish(share(grad_rows, acts[0], acts[1]))
    grad_gate = finish(share(hidden2, dgates[0], dgates[1]))
    grad_up = finish(share(hidden2, dups[0], dups[1]))

    mixed_rows = plane.turn(mixed)
    grad_output = finish(share(da, mixed_rows[:, :head_cols], mixed_rows[:, head_cols:]))
    dout = plane.turn(dot_plain(da, wo).astype(BF))
    dquery, dkey, dvalue, dkey_edge, dvalue_edge = attend_back(
        query, key, value, halo, first, lse, dout, cos_tab, sin_tab
    )
    edges = jnp.concatenate(
        [
            dkey_edge[:, head_cols:],
            dkey_edge[:, :head_cols],
            dvalue_edge[:, head_cols:],
            dvalue_edge[:, :head_cols],
        ],
        axis=1,
    )
    edges = lax.ppermute(edges, ("fsdp", "tp"), backward)
    edges = jnp.pad(edges, ((rows - HALO, 0), (0, 0))).astype(F32)
    local = 2 * head_cols
    dkey = (dkey + edges[:, :local]).astype(BF)
    dvalue = (dvalue + edges[:, local:]).astype(BF)
    own, oth = slice(0, head_cols), slice(head_cols, local)
    d_own = jnp.concatenate([dquery[:, own], dkey[:, own], dvalue[:, own]], axis=1)
    d_oth = jnp.concatenate([dquery[:, oth], dkey[:, oth], dvalue[:, oth]], axis=1)
    qkv_own, qkv_oth = attn_own[:, : 3 * head_cols], attn_oth[:, : 3 * head_cols]
    dh1 = plane.turn(
        jnp.concatenate([d_own, d_oth], axis=1)
    )
    dh1 = dot_last(dh1[:, : 3 * head_cols], qkv_own) + dot_last(dh1[:, 3 * head_cols :], qkv_oth)
    normed1, inv_dev1 = normalize(resid)
    dx = dx1 + norm_back(scatter(dh1), normed1, inv_dev1)
    input_grad = plane.to_blocks(dx.astype(BF))

    grads_qkv = share(hidden1, d_own, d_oth)
    grad_query, grad_key, grad_value = (
        finish(grads_qkv[:, i * head_cols : (i + 1) * head_cols]) for i in range(3)
    )
    return (
        layer_out, input_grad, grad_query, grad_key, grad_value, grad_output,
        grad_gate, grad_up, grad_down,
    )


def solution(mesh):
    rows = P(("fsdp", "ctx"), "tp")
    weight = P("fsdp", "tp")
    return jax.shard_map(
        body,
        mesh=mesh,
        in_specs=(rows, rows, P(), P()) + (weight,) * 7,
        out_specs=(rows, rows) + (weight,) * 7,
        check_vma=False,
    )
```

```python
import functools
import math

import jax
import jax.numpy as jnp
from jax import lax
from jax.experimental import pallas as pl
from jax.experimental.pallas import tpu as pltpu
from jax.sharding import PartitionSpec as P

HD = 128
HALO = 1024
EPSILON = 1e-05
NEG_FILL = -1e30
PLANE = ("ctx", "tp")
BF = jnp.bfloat16
F32 = jnp.float32


def takes(microseconds):
    return pl.CostEstimate(
        flops=int(microseconds * 30e6), bytes_accessed=1, transcendentals=0
    )


def dot_plain(left, right):
    return jnp.dot(left, right, preferred_element_type=F32)


def dot_last(left, right):
    return lax.dot_general(left, right, (((1,), (1,)), ((), ())), preferred_element_type=F32)


def dot_rows(left, right):
    return lax.dot_general(left, right, (((0,), (0,)), ((), ())), preferred_element_type=F32)


def normalize(values):
    average = jnp.mean(values, axis=-1, keepdims=True)
    centred = values - average
    spread = jnp.mean(centred * centred, axis=-1, keepdims=True)
    inv_dev = lax.rsqrt(spread + EPSILON)
    return (centred * inv_dev, inv_dev)


def norm_back(grad, normed, inv_dev):
    grad_mean = jnp.mean(grad, axis=-1, keepdims=True)
    cross_mean = jnp.mean(grad * normed, axis=-1, keepdims=True)
    return inv_dev * (grad - grad_mean - normed * cross_mean)


def slots(lengths, order):
    seq_len = lengths.reshape(-1)
    seq_ids = jnp.arange(seq_len.shape[0], dtype=jnp.int32)
    picks = order[:, None] == seq_ids[None, :]
    order_len = jnp.sum(jnp.where(picks, seq_len[None, :], 0), axis=1)
    return jnp.cumsum(order_len) - order_len


def first_of(index, starts):
    inside = index[:, None] >= starts[None, :]
    return jnp.max(jnp.where(inside, starts[None, :], 0), axis=1)


def qkv_kernel(heads, table, *refs):
    *pieces, own_ref, oth_ref, cos_ref, sin_ref, x_ref, h_ref, q_ref, k_ref, v_ref, e_ref = refs
    cols = pieces[0].shape[1]
    for i, piece in enumerate(pieces):
        x_ref[:, pl.ds(pl.multiple_of(table[i] * cols, cols), cols)] = piece[...]
    values = x_ref[...].astype(F32)
    normed, _ = normalize(values)
    hidden = normed.astype(BF)
    h_ref[...] = hidden
    cos, sin = cos_ref[...], sin_ref[...]
    width = heads * HD
    for piece, w_ref in enumerate((own_ref, oth_ref)):
        out = dot_plain(hidden, w_ref[...])
        for head in range(heads):
            to = (piece * heads + head) * HD
            swapped = ((1 - piece) * heads + head) * HD
            query = out[:, head * HD : (head + 1) * HD]
            key = out[:, width + head * HD : width + (head + 1) * HD]
            value = out[:, 2 * width + head * HD : 2 * width + (head + 1) * HD].astype(BF)
            query = (query * cos + pltpu.roll(query, HD // 2, 1) * sin).astype(BF)
            key = (key * cos + pltpu.roll(key, HD // 2, 1) * sin).astype(BF)
            q_ref[:, to : to + HD] = query
            k_ref[:, to : to + HD] = key
            v_ref[:, to : to + HD] = value
            e_ref[:, swapped : swapped + HD] = key
            e_ref[:, 2 * width + swapped : 2 * width + swapped + HD] = value


def project(pieces, places, w_own, w_oth, cos_tab, sin_tab, heads):
    rows, cols = pieces[0].shape
    width = cols * len(pieces)
    block = rows // 3
    skip = rows // block - HALO // block
    local = 2 * heads * HD
    row = lambda i, t: (i, 0)
    once = pl.BlockSpec((width, 3 * heads * HD), lambda i, t: (0, 0))
    table = pl.BlockSpec((block, HD), lambda i, t: (i + HALO // block, 0))
    part = pl.BlockSpec((block, local), row)
    return pl.pallas_call(
        functools.partial(qkv_kernel, heads),
        grid_spec=pltpu.PrefetchScalarGridSpec(
            num_scalar_prefetch=1,
            grid=(rows // block,),
            in_specs=[pl.BlockSpec((block, cols), row)] * len(pieces) + [once, once, table, table],
            out_specs=[pl.BlockSpec((block, width), row)] * 2
            + [part] * 3
            + [pl.BlockSpec((block, 2 * local), lambda i, t: (jnp.maximum(i - skip, 0), 0))],
        ),
        out_shape=[jax.ShapeDtypeStruct((rows, width), BF)] * 2
        + [jax.ShapeDtypeStruct((rows, local), BF)] * 3
        + [jax.ShapeDtypeStruct((HALO, 2 * local), BF)],
        cost_estimate=takes(20),
        name="norm_project",
    )(jnp.stack([jnp.asarray(p, jnp.int32) for p in places]), *pieces, w_own, w_oth, cos_tab, sin_tab)


def join_kernel(table, *refs):
    *pieces, out_ref = refs
    cols = pieces[0].shape[1]
    for i, piece in enumerate(pieces):
        out_ref[:, pl.ds(pl.multiple_of(table[i] * cols, cols), cols)] = piece[...]


def join(pieces, places, chunks):
    rows, cols = pieces[0].shape
    count, ranks = len(pieces), len(chunks)
    chunk = rows // ranks
    table = jnp.stack([jnp.asarray(v, jnp.int32) for v in list(places) + list(chunks)])
    piece = pl.BlockSpec((chunk, cols), lambda i, t: (t[count + i], 0))
    return pl.pallas_call(
        join_kernel,
        grid_spec=pltpu.PrefetchScalarGridSpec(
            num_scalar_prefetch=1,
            grid=(ranks,),
            in_specs=[piece] * count,
            out_specs=pl.BlockSpec((chunk, cols * count), lambda i, t: (i, 0)),
        ),
        out_shape=jax.ShapeDtypeStruct((rows, cols * count), pieces[0].dtype),
        cost_estimate=takes(5),
        name="join",
    )(table, *pieces)


def pack_kernel(table, *refs):
    *ins, out_ref = refs
    at = 0
    for ref in ins:
        out_ref[:, at : at + ref.shape[1]] = ref[...]
        at += ref.shape[1]


def pack(weights, c, at, size, steps):
    rows = weights[0].shape[0]
    cols = weights[0].shape[1] // 2
    table = jnp.asarray(c, jnp.int32).reshape(1)
    spec = pl.BlockSpec((rows, size), lambda n, t: (0, t[0] * (cols // size) + at // size + n))
    return pl.pallas_call(
        pack_kernel,
        grid_spec=pltpu.PrefetchScalarGridSpec(
            num_scalar_prefetch=1,
            grid=(steps,),
            in_specs=[spec] * len(weights),
            out_specs=pl.BlockSpec((rows, size * len(weights)), lambda n, t: (0, n)),
        ),
        out_shape=jax.ShapeDtypeStruct((rows, size * len(weights) * steps), weights[0].dtype),
        cost_estimate=takes(2),
        name="pack",
    )(table, *weights)


def allowed_keys(first_ref, step, block):
    span = block + HALO
    keys = lax.broadcasted_iota(jnp.int32, (block, span), 1)
    rows = lax.broadcasted_iota(jnp.int32, (block, span), 0)
    first = first_ref[...] - step * block
    return (keys >= first) & (keys <= rows + HALO)


def attend_kernel(late, base, q_ref, k_ref, v_ref, *refs):
    if late:
        first_ref, o_ref, lse_ref = refs
    else:
        ke_ref, ve_ref, first_ref, _, _, o_ref, lse_ref, keys, values = refs
    step = pl.program_id(1) + base
    block = q_ref.shape[0]
    if late:
        window = pl.ds(pl.multiple_of(step * block - HALO, block), block + HALO)
        key, value = k_ref[window, :], v_ref[window, :]
    else:

        @pl.when(pl.program_id(1) == 0)
        def _():
            keys[:HALO] = ke_ref[...]
            keys[HALO:] = k_ref[...]
            values[:HALO] = ve_ref[...]
            values[HALO:] = v_ref[...]

        window = pl.ds(pl.multiple_of(step * block, block), block + HALO)
        key, value = keys[window, :], values[window, :]
    raw = dot_last(q_ref[...], key) * (HD**-0.5)
    raw = jnp.where(allowed_keys(first_ref, step, block), raw, NEG_FILL)
    top = jnp.max(raw, axis=-1, keepdims=True)
    expo = jnp.exp(raw - top)
    denom = jnp.sum(expo, axis=-1, keepdims=True)
    probs = (expo * (1.0 / denom)).astype(BF)
    o_ref[...] = dot_plain(probs, value).astype(BF)
    lse_ref[...] = top + jnp.log(denom)


def attend(q, k, v, halo, first, done=None, block=256):
    rows, local = q.shape
    heads = local // HD
    late = halo is None
    base = HALO // block if late else 0
    steps = rows // block - base if late else HALO // block
    row = pl.BlockSpec((block, HD), lambda h, i: (base + i, h))
    column = pl.BlockSpec((rows, HD), lambda h, i: (0, h))
    bound = pl.BlockSpec((block, 1), lambda h, i: (base + i, 0))
    norm = pl.BlockSpec((None, block, 1), lambda h, i: (h, base + i, 0))
    if late:
        in_specs, operands, scratch, aliases = [row, column, column, bound], (q, k, v, first), [], {}
    else:
        edge = [pl.BlockSpec((HALO, HD), lambda h, i, at=at: (0, h + at)) for at in (0, heads)]
        whole = pl.BlockSpec(memory_space=pl.ANY)
        in_specs = [row, column, column] + edge + [bound, whole, whole]
        operands = (q, k, v, halo, halo, first) + tuple(done)
        scratch = [pltpu.VMEM((HALO + rows, HD), BF)] * 2
        aliases = {6: 0, 7: 1}
    return pl.pallas_call(
        functools.partial(attend_kernel, late, base),
        grid=(heads, steps),
        in_specs=in_specs,
        out_specs=[row, norm],
        out_shape=[
            jax.ShapeDtypeStruct((rows, local), BF),
            jax.ShapeDtypeStruct((heads, rows, 1), F32),
        ],
        scratch_shapes=scratch,
        input_output_aliases=aliases,
        cost_estimate=takes(10 if late else 20),
        name="attend_late" if late else "attend_early",
    )(*operands)


def rotate_back(grad, cos, sin):
    return grad * cos - pltpu.roll(grad, HD // 2, 1) * sin


def attend_back_kernel(
    q_ref, k_ref, v_ref, ke_ref, ve_ref, first_ref, lse_ref, do_ref, cos_ref, sin_ref,
    dq_ref, dk_ref, dv_ref, e_ref, keys, values, dkeys, dvalues,
):
    step = pl.program_id(1)
    block = q_ref.shape[0]
    scale = HD**-0.5

    @pl.when(step == 0)
    def _():
        keys[:HALO] = ke_ref[...]
        keys[HALO:] = k_ref[...]
        values[:HALO] = ve_ref[...]
        values[HALO:] = v_ref[...]
        dkeys[...] = jnp.zeros_like(dkeys)
        dvalues[...] = jnp.zeros_like(dvalues)

    window = pl.ds(pl.multiple_of(step * block, block), block + HALO)
    query, dout = q_ref[...], do_ref[...]
    raw = dot_last(query, keys[window, :]) * scale
    probs = jnp.where(allowed_keys(first_ref, step, block), jnp.exp(raw - lse_ref[...]), 0.0)
    dprob = dot_last(dout, values[window, :])
    delta = jnp.sum(probs * dprob, axis=-1, keepdims=True)
    dscore = (probs * (dprob - delta)).astype(BF)
    mine = pl.ds(pl.multiple_of(HALO + step * block, block), block)
    dquery = dot_plain(dscore, keys[window, :]) * scale
    dq_ref[...] = rotate_back(dquery, cos_ref[mine, :], sin_ref[mine, :]).astype(BF)
    dkeys[window, :] += dot_rows(dscore, query)
    dvalues[window, :] += dot_rows(probs.astype(BF), dout)

    @pl.when(step == pl.num_programs(1) - 1)
    def _():
        dkey = rotate_back(dkeys[...] * scale, cos_ref[...], sin_ref[...])
        e_ref[0] = dkey[:HALO].astype(BF)
        dk_ref[...] = dkey[HALO:]
        e_ref[1] = dvalues[:HALO].astype(BF)
        dv_ref[...] = dvalues[HALO:]


def attend_back(q, k, v, halo, first, lse, dout, cos_tab, sin_tab, block=256):
    rows, local = q.shape
    heads = local // HD
    span = block + HALO
    column = pl.BlockSpec((rows, HD), lambda h, i: (0, h))
    piece = pl.BlockSpec((block, HD), lambda h, i: (i, h))
    table = pl.BlockSpec((HALO + rows, HD), lambda h, i: (0, 0))
    edge = pl.BlockSpec((HALO, HD), lambda h, i: (0, h))
    return pl.pallas_call(
        attend_back_kernel,
        grid=(heads, rows // block),
        in_specs=[
            piece,
            column,
            column,
            edge,
            pl.BlockSpec((HALO, HD), lambda h, i: (0, h + heads)),
            pl.BlockSpec((block, 1), lambda h, i: (i, 0)),
            pl.BlockSpec((None, block, 1), lambda h, i: (h, i, 0)),
            piece,
            table,
            table,
        ],
        out_specs=[
            piece,
            column,
            column,
            pl.BlockSpec((2, HALO, HD), lambda h, i: (0, 0, (h + heads // 2) % heads)),
        ],
        out_shape=[
            jax.ShapeDtypeStruct((rows, local), BF),
            jax.ShapeDtypeStruct((rows, local), F32),
            jax.ShapeDtypeStruct((rows, local), F32),
            jax.ShapeDtypeStruct((2, HALO, local), BF),
        ],
        scratch_shapes=[pltpu.VMEM((HALO + rows, HD), BF)] * 2
        + [pltpu.VMEM((HALO + rows, HD), F32)] * 2,
        cost_estimate=takes(43),
        name="attend_back",
    )(q, k, v, halo, halo, first, lse, dout, cos_tab, sin_tab)


def ffn_kernel(first_half, seeded, shared_count, table, h_ref, g_ref, own_ref, oth_ref, *refs):
    count = 2 if not first_half else int(seeded)
    starts, refs = refs[:count], refs[count + shared_count :]
    back_ref, act_own, act_oth, d_own, d_oth, *outs, back, forth = refs
    step = pl.program_id(0)
    hidden, grad = h_ref[...], g_ref[...]
    size = own_ref.shape[1] // 3

    @pl.when(step == 0)
    def _():
        if first_half:
            outs[1][...] = hidden
            back[...] = jnp.zeros_like(back)
            forth[...] = starts[0][...] if seeded else jnp.zeros_like(forth)
        else:
            back[...] = starts[0][...]
            forth[...] = starts[1][...]

    for w_ref, act_ref, d_ref in ((own_ref, act_own, d_own), (oth_ref, act_oth, d_oth)):
        both = dot_plain(hidden, w_ref[:, : 2 * size])
        dact = dot_plain(grad, w_ref[:, 2 * size :]).astype(BF).astype(F32)
        gate, up = both[:, :size], both[:, size:]
        sig = jax.nn.sigmoid(gate)
        silu = gate * sig
        act = (silu * up).astype(BF)
        dgate = (dact * up * sig * (1.0 + gate * (1.0 - sig))).astype(BF)
        dup = (dact * silu).astype(BF)
        act_ref[...] = act
        d_ref[:, :size] = dgate
        d_ref[:, size:] = dup
        forth[...] += dot_last(act, w_ref[:, 2 * size :])
        back[...] += dot_last(d_ref[...], w_ref[:, : 2 * size])

    @pl.when(step == pl.num_programs(0) - 1)
    def _():
        back_ref[...] = back[...].astype(back_ref.dtype)
        if first_half:
            outs[0][...] = forth[...]
        else:
            for i, out_ref in enumerate(outs):
                cols = out_ref.shape[1]
                at = pl.multiple_of(table[1 + i] * cols, cols)
                out_ref[...] = forth[:, pl.ds(at, cols)].astype(BF)


def feed_forward(j, place, places, hidden, grad_rows, w_own, w_oth, half, size, starts, shared, kind):
    chunk, width = hidden.shape
    rows = grad_rows.shape[0]
    first_half = places is None
    steps = half // size
    fixed = pl.BlockSpec((chunk, width), lambda n, t: (0, 0))
    at_j = pl.BlockSpec((chunk, width), lambda n, t: (j, 0))
    weight = pl.BlockSpec((width, 3 * size), lambda n, t: (0, n))
    table = jnp.stack([jnp.asarray(p, jnp.int32) for p in [place] + list(places or [])])
    starts = [] if starts is None else list(starts)
    operands = [hidden, grad_rows, w_own, w_oth] + starts
    in_specs = [fixed, at_j, weight, weight] + [fixed] * len(starts)
    act = pl.BlockSpec((chunk, size), lambda n, t: (j, n))
    both = pl.BlockSpec((chunk, 2 * size), lambda n, t: (j, n))
    out_specs = [fixed, act, act, both, both]
    out_shape = (
        [jax.ShapeDtypeStruct((chunk, width), kind)]
        + [jax.ShapeDtypeStruct((rows, half), BF)] * 2
        + [jax.ShapeDtypeStruct((rows, 2 * half), BF)] * 2
    )
    shared_at = [1, 2, 3, 4]
    if first_half:
        out_specs += [fixed, at_j]
        out_shape += [
            jax.ShapeDtypeStruct((chunk, width), F32),
            jax.ShapeDtypeStruct((rows, width), BF),
        ]
        shared_at.append(6)
    else:
        cols = width // len(places)
        out_specs += [pl.BlockSpec((chunk, cols), lambda n, t: (t[0], 0))] * len(places)
        out_shape += [jax.ShapeDtypeStruct((rows, cols), BF)] * len(places)
        shared_at += [5 + i for i in range(len(places))]
    aliases = {}
    if shared is not None:
        aliases = {1 + len(operands) + i: at for i, at in enumerate(shared_at)}
        in_specs += [pl.BlockSpec(memory_space=pl.ANY)] * len(shared)
        operands += list(shared)
    out = pl.pallas_call(
        functools.partial(
            ffn_kernel, first_half, len(starts) == 1, 0 if shared is None else len(shared)
        ),
        grid_spec=pltpu.PrefetchScalarGridSpec(
            num_scalar_prefetch=1,
            grid=(steps,),
            in_specs=in_specs,
            out_specs=out_specs,
            scratch_shapes=[pltpu.VMEM((chunk, width), F32)] * 2,
        ),
        out_shape=out_shape,
        input_output_aliases=aliases,
        cost_estimate=takes(20),
        compiler_params=pltpu.CompilerParams(vmem_limit_bytes=60 << 20),
        name="feed_forward",
    )(table, *operands)
    sums = [out[0], out[5]] if first_half else out[0]
    return sums, [out[at] for at in shared_at]


def finish_kernel(dq, dk, dv, e_ref, d_own, d_oth, edges):
    step = pl.program_id(0)
    chunk, local = dq.shape
    lead = edges.shape[1] - e_ref.shape[1]

    @pl.when(step == 0)
    def _():
        edges[:, :lead] = jnp.zeros((2, lead, local), BF)
        edges[:, lead:] = e_ref[...]

    rows = pl.ds(pl.multiple_of(step * chunk, chunk), chunk)
    dkey = (dk[...] + edges[0, rows, :].astype(F32)).astype(BF)
    dvalue = (dv[...] + edges[1, rows, :].astype(F32)).astype(BF)
    cols = local // 2
    for ref, at in ((d_own, 0), (d_oth, cols)):
        ref[:, :cols] = dq[:, at : at + cols]
        ref[:, cols : 2 * cols] = dkey[:, at : at + cols]
        ref[:, 2 * cols :] = dvalue[:, at : at + cols]


def finish_attention(dq, dk, dv, edges, block=256):
    rows, local = dq.shape
    inner = 3 * local // 2
    row = lambda i: (i, 0)
    part = pl.BlockSpec((block, local), row)
    return pl.pallas_call(
        finish_kernel,
        grid=(rows // block,),
        in_specs=[part, part, part, pl.BlockSpec(edges.shape, lambda i: (0, 0, 0))],
        out_specs=[pl.BlockSpec((block, inner), row)] * 2,
        out_shape=[jax.ShapeDtypeStruct((rows, inner), BF)] * 2,
        scratch_shapes=[pltpu.VMEM((2, rows, local), BF)],
        cost_estimate=takes(4),
        name="finish_attention",
    )(dq, dk, dv, edges)


def input_kernel(table, d_own, d_oth, w_own, w_oth, x_ref, dx_ref, *outs):
    step = pl.program_id(0)
    grad = dot_last(d_own[...], w_own[...]) + dot_last(d_oth[...], w_oth[...])
    normed, inv_dev = normalize(x_ref[...].astype(F32))
    grad = norm_back(grad, normed, inv_dev)
    keep = jnp.where(step == table[0], 1.0, 0.0)
    grad = (grad + keep * dx_ref[...]).astype(BF)
    for i, out_ref in enumerate(outs):
        width = out_ref.shape[1]
        for t in range(len(outs)):

            @pl.when(table[1 + i] == t)
            def _():
                out_ref[...] = grad[:, t * width : (t + 1) * width]


def input_parts(rank, places, d_own, d_oth, w_own, w_oth, full_x, dx1):
    rows, width = full_x.shape
    chunk = dx1.shape[0]
    inner = w_own.shape[1]
    cols = width // len(places)
    row = lambda i, t: (i, 0)
    once = lambda i, t: (0, 0)
    return pl.pallas_call(
        input_kernel,
        grid_spec=pltpu.PrefetchScalarGridSpec(
            num_scalar_prefetch=1,
            grid=(rows // chunk,),
            in_specs=[
                pl.BlockSpec((chunk, inner), row),
                pl.BlockSpec((chunk, inner), row),
                pl.BlockSpec((width, inner), once),
                pl.BlockSpec((width, inner), once),
                pl.BlockSpec((chunk, width), row),
                pl.BlockSpec((chunk, width), once),
            ],
            out_specs=[pl.BlockSpec((chunk, cols), row)] * len(places),
        ),
        out_shape=[jax.ShapeDtypeStruct((rows, cols), BF)] * len(places),
        cost_estimate=takes(20),
        compiler_params=pltpu.CompilerParams(vmem_limit_bytes=60 << 20),
        name="input_parts",
    )(
        jnp.stack([jnp.asarray(p, jnp.int32) for p in [rank] + list(places)]),
        d_own, d_oth, w_own, w_oth, full_x, dx1,
    )


def shares_kernel(table, m_ref, w_own, w_oth, keep_ref, mine_ref, *refs):
    cols = w_own.shape[1]
    keep_ref[...] = m_ref[...]
    out = dot_last(m_ref[:, :cols], w_own[...]) + dot_last(m_ref[:, cols:], w_oth[...])
    for j, ref in enumerate((mine_ref,) + refs):

        @pl.when(pl.program_id(0) == j)
        def _():
            ref[...] = out.astype(ref.dtype)


def output_shares(mixed, w_own, w_oth, turned):
    rows, local = mixed.shape
    width, cols = w_own.shape
    ranks = len(turned)
    chunk = rows // ranks
    once = lambda j, t: (0, 0)
    return pl.pallas_call(
        shares_kernel,
        grid_spec=pltpu.PrefetchScalarGridSpec(
            num_scalar_prefetch=1,
            grid=(ranks,),
            in_specs=[
                pl.BlockSpec((chunk, local), lambda j, t: (t[j], 0)),
                pl.BlockSpec((width, cols), once),
                pl.BlockSpec((width, cols), once),
            ],
            out_specs=[pl.BlockSpec((chunk, local), lambda j, t: (j, 0))]
            + [pl.BlockSpec((chunk, width), once)] * ranks,
        ),
        out_shape=[
            jax.ShapeDtypeStruct((rows, local), BF),
            jax.ShapeDtypeStruct((chunk, width), F32),
        ]
        + [jax.ShapeDtypeStruct((chunk, width), BF)] * (ranks - 1),
        cost_estimate=takes(7),
        compiler_params=pltpu.CompilerParams(vmem_limit_bytes=60 << 20),
        name="output_shares",
    )(jnp.stack(turned).astype(jnp.int32), mixed, w_own, w_oth)


def dmixed_kernel(table, *refs):
    *chunks, w_own, w_oth, keep_ref, d_ref = refs
    cols = w_own.shape[1]
    for j in range(len(chunks)):

        @pl.when(pl.program_id(0) == j)
        def _():
            chunk = chunks[j][...]
            keep_ref[...] = chunk
            d_ref[:, :cols] = dot_plain(chunk, w_own[...]).astype(BF)
            d_ref[:, cols:] = dot_plain(chunk, w_oth[...]).astype(BF)


def dmixed(chunks, w_own, w_oth, turned):
    chunk, width = chunks[0].shape
    cols = w_own.shape[1]
    ranks = len(chunks)
    once = lambda j, t: (0, 0)
    return pl.pallas_call(
        dmixed_kernel,
        grid_spec=pltpu.PrefetchScalarGridSpec(
            num_scalar_prefetch=1,
            grid=(ranks,),
            in_specs=[pl.BlockSpec((chunk, width), once)] * ranks
            + [pl.BlockSpec((width, cols), once)] * 2,
            out_specs=[
                pl.BlockSpec((chunk, width), lambda j, t: (j, 0)),
                pl.BlockSpec((chunk, 2 * cols), lambda j, t: (t[j], 0)),
            ],
        ),
        out_shape=[
            jax.ShapeDtypeStruct((chunk * ranks, width), BF),
            jax.ShapeDtypeStruct((chunk * ranks, 2 * cols), BF),
        ],
        cost_estimate=takes(7),
        compiler_params=pltpu.CompilerParams(vmem_limit_bytes=60 << 20),
        name="dmixed",
    )(jnp.stack(turned).astype(jnp.int32), *chunks, w_own, w_oth)


def norm_kernel(table, x_ref, mine_ref, *refs):
    *others, resid_ref, h_ref = refs
    total = x_ref[...].astype(F32) + mine_ref[...]
    for ref in others:
        total = total + ref[...].astype(F32)
    resid_ref[...] = total
    h_ref[...] = normalize(total)[0].astype(BF)


def norm_chunk(rank, full_x, mine, others):
    chunk, width = mine.shape
    block = chunk // 3
    row = pl.BlockSpec((block, width), lambda i, t: (i, 0))
    return pl.pallas_call(
        norm_kernel,
        grid_spec=pltpu.PrefetchScalarGridSpec(
            num_scalar_prefetch=1,
            grid=(3,),
            in_specs=[pl.BlockSpec((block, width), lambda i, t: (t[0] * 3 + i, 0)), row]
            + [row] * len(others),
            out_specs=[row, row],
        ),
        out_shape=[
            jax.ShapeDtypeStruct((chunk, width), F32),
            jax.ShapeDtypeStruct((chunk, width), BF),
        ],
        cost_estimate=takes(4),
        name="norm_chunk",
    )(jnp.asarray(rank, jnp.int32).reshape(1), full_x, mine, *others)


def back_kernel(g_ref, resid_ref, mine_ref, *refs):
    *others, dx_ref, da_ref = refs
    total = mine_ref[...]
    for ref in others:
        total = total + ref[...].astype(F32)
    normed, inv_dev = normalize(resid_ref[...])
    dx = g_ref[...].astype(F32) + norm_back(total, normed, inv_dev)
    dx_ref[...] = dx
    da_ref[...] = dx.astype(BF)


def back_chunk(grad_rows, resid1, mine, others):
    chunk, width = mine.shape
    block = chunk // 3
    row = pl.BlockSpec((block, width), lambda i: (i, 0))
    return pl.pallas_call(
        back_kernel,
        grid=(3,),
        in_specs=[row] * (3 + len(others)),
        out_specs=[row, row],
        out_shape=[
            jax.ShapeDtypeStruct((chunk, width), F32),
            jax.ShapeDtypeStruct((chunk, width), BF),
        ],
        cost_estimate=takes(4),
        name="back_chunk",
    )(grad_rows, resid1, mine, *others)


def grads_kernel(count, *refs):
    *ins, out_ref = refs
    at = 0
    for left, right in zip(ins[:count], ins[count : 2 * count]):
        cols = right.shape[1]
        total = dot_rows(left[...], right[...])
        if len(ins) > 2 * count:
            total = total + ins[-1][:, at : at + cols].astype(F32)
        out_ref[:, at : at + cols] = total.astype(BF)
        at += cols


def grads(lefts, rights, other=None):
    rows, width = lefts[0].shape
    cols = sum(r.shape[1] for r in rights)
    block = 512
    in_specs = [pl.BlockSpec((rows, block), lambda m: (0, m))] * len(lefts)
    in_specs += [pl.BlockSpec(r.shape, lambda m: (0, 0)) for r in rights]
    out = pl.BlockSpec((block, cols), lambda m: (m, 0))
    operands = list(lefts) + list(rights)
    if other is not None:
        in_specs.append(out)
        operands.append(other)
    return pl.pallas_call(
        functools.partial(grads_kernel, len(lefts)),
        grid=(width // block,),
        in_specs=in_specs,
        out_specs=out,
        out_shape=jax.ShapeDtypeStruct((width, cols), BF),
        cost_estimate=takes(10),
        compiler_params=pltpu.CompilerParams(vmem_limit_bytes=60 << 20),
        name="grads",
    )(*operands)


def after(value, *others):
    return lax.optimization_barrier((value,) + others)[0]


class Plane:
    def __init__(self):
        self.nc, self.nt = lax.axis_size("ctx"), lax.axis_size("tp")
        assert self.nc == 2 and self.nt % 2 == 0
        self.hi = self.nt // self.nc
        self.ranks = self.nc * self.hi
        tp_place = lax.axis_index("tp")
        self.c = lax.axis_index("ctx")
        self.h, self.k = tp_place // self.nc, tp_place % self.nc
        self.r = self.c * self.hi + self.h

    def perm(self, move):
        pairs = []
        for c in range(self.nc):
            for h in range(self.hi):
                for k in range(self.nc):
                    c2, h2, k2 = move(c, h, k)
                    pairs.append((c * self.nt + h * self.nc + k, c2 * self.nt + h2 * self.nc + k2))
        return pairs

    def spread_rows(self, block):
        got = []
        for jh in range(self.hi):
            for jk in range(self.nc):
                move = lambda c, h, k: (k ^ jk, h ^ jh, c)
                place = (self.h ^ jh) * self.nc + (self.c ^ jk)
                got.append((place, lax.ppermute(block, PLANE, self.perm(move))))
        return got

    def block_places(self):
        return [
            (self.h ^ jh) * self.nc + (self.c ^ jk) for jh in range(self.hi) for jk in range(self.nc)
        ]

    def collect_blocks(self, pieces):
        moves = [
            lambda c, h, k, jh=jh, jk=jk: (k, h ^ jh, c ^ jk)
            for jh in range(self.hi)
            for jk in range(self.nc)
        ]
        return [lax.ppermute(p, PLANE, self.perm(m)) for p, m in zip(pieces, moves)]

    def swap(self, value, j):
        def move(c, h, k):
            rank = (c * self.hi + h) ^ j
            return rank // self.hi, rank % self.hi, k

        return lax.ppermute(value, PLANE, self.perm(move))

    def chunk_of(self, value, j):
        size = value.shape[0] // self.ranks
        return lax.dynamic_slice_in_dim(value, (self.r ^ j) * size, size, 0)

    def turn(self, value):
        return jnp.concatenate([self.chunk_of(value, j) for j in range(self.ranks)], axis=0)

    def gather(self, mine, use=None):
        use = use or (lambda j, chunk: chunk[:8, :128])
        out = [mine]
        if self.ranks != 4:
            out += [self.swap(mine, j) for j in range(1, self.ranks)]
            for j in range(self.ranks):
                use(j, out[j])
            return out
        near, far = self.swap(mine, 1), self.swap(mine, 2)
        near, far, _ = lax.optimization_barrier((near, far, use(0, mine)))
        half = mine.shape[0] // 2
        corner = [self.swap(near[:half], 2), self.swap(far[half:], 1)]
        use(1, near)
        last = use(2, far)
        corner = jnp.concatenate(lax.optimization_barrier((*corner, last))[:2], axis=0)
        use(3, corner)
        return [mine, near, far, corner]

    def pair(self, value):
        perm = [(t, t ^ 1) for t in range(self.nt)]
        return lax.ppermute(value, "tp", perm)


def body(
    tokens, cotangent, lengths, order, w_query, w_key, w_value, w_output, w_gate, w_up, w_down
):
    plane = Plane()
    rows = tokens.shape[0]
    nf, nc, nt, ranks = lax.axis_size("fsdp"), plane.nc, plane.nt, plane.ranks
    z = lax.axis_index("fsdp")
    chunk = rows // ranks
    head_cols = w_query.shape[1] // nc
    heads = head_cols // HD
    hidden_cols = w_gate.shape[1] // nc
    half = hidden_cols // 2
    size = min(256, half)

    def over_fsdp(shard):
        return lax.all_gather(shard, "fsdp", axis=0, tiled=True)

    fence = lambda *values: lax.optimization_barrier(values)
    turned = [plane.r ^ j for j in range(ranks)]

    qkv_own = over_fsdp(pack((w_query, w_key, w_value), plane.c, 0, head_cols, 1))
    places, got_x = zip(*plane.spread_rows(tokens))
    base = (z * nc + plane.k) * rows - HALO
    index = base + jnp.arange(HALO + rows, dtype=jnp.int32)
    starts = first_of(index, slots(lengths, order))
    within = index - starts
    first = (starts[HALO:] - base)[:, None]
    lane = jnp.arange(HD, dtype=jnp.int32)
    freq = jnp.exp((lane % (HD // 2)).astype(F32) * (-2.0 * math.log(10000.0) / HD))
    angle = within.astype(F32)[:, None] * freq[None, :]
    cos_tab = jnp.cos(angle)
    sin_tab = jnp.sin(angle) * jnp.where(lane < HD // 2, -1.0, 1.0)[None, :]
    qkv_own, cos_tab, sin_tab, first, *got_x = fence(qkv_own, cos_tab, sin_tab, first, *got_x)
    qkv_oth = plane.pair(qkv_own)
    w_output, cotangent = fence(w_output, cotangent, *got_x)[:2]
    wo_own = over_fsdp(pack((w_output,), plane.c, 0, head_cols, 1))
    _, got_g = zip(*plane.spread_rows(cotangent))

    full_x, hidden1, query, key, value, edge = project(
        got_x, places, qkv_own, qkv_oth, cos_tab, sin_tab, heads
    )
    onward = []
    for f in range(nf):
        for h in range(plane.hi):
            for k in range(nc):
                to = f * nc + k + 1
                if to < nf * nc:
                    onward.append((f * nt + h * nc + k, to // nc * nt + h * nc + to % nc))
    backward = [(b, a) for a, b in onward]
    halo = lax.ppermute(edge, ("fsdp", "tp"), onward)
    wo_oth = plane.pair(after(wo_own, edge))
    late = attend(query, key, value, None, first)
    halo, wo_own, wo_oth, *late = fence(halo, wo_own, wo_oth, *late)
    own0 = over_fsdp(
        pack(after((w_gate, w_up, w_down), halo), plane.c, 0, size, half // size)
    )
    mixed, lse = attend(query, key, value, halo, first, late)

    mixed_rows, mine, *shares = output_shares(mixed, wo_own, wo_oth, turned)
    sent = [plane.swap(shares[j - 1], j) for j in range(ranks - 1, 0, -1)]
    mine, *got_g = fence(mine, *got_g)
    grad_rows = join(got_g, places, turned)
    shard1 = pack(after((w_gate, w_up, w_down), mine), plane.c, half, size, half // size)
    own1 = over_fsdp(shard1)
    mine, grad_rows, *sent = fence(mine, grad_rows, *sent, shard1)[:-1]
    resid1, mine = norm_chunk(plane.r, full_x, mine, sent)
    oth0 = plane.pair(after(own0, mine))

    sums, shared = {}, None

    def first_half(j, piece):
        nonlocal shared
        sums[j], shared = feed_forward(
            j, turned[j], None, piece, grad_rows, own0, oth0, half, size,
            None if j else [resid1], shared, F32,
        )
        return sums[j][0]

    pieces = plane.gather(mine, first_half)
    act_own, act_oth, d_own, d_oth, hidden2 = shared

    def halves(lefts, rights_own, rights_oth):
        return grads(lefts, rights_own, plane.pair(grads(lefts, rights_oth)))

    def reduce_rows(total):
        return lax.psum_scatter(total, "fsdp", scatter_dimension=0, tiled=True)

    def exchange(mine):
        return lax.ppermute(mine, "ctx", [(0, 1), (1, 0)])

    def both_parts(mine, other):
        here = plane.c == 0
        return jnp.where(here, mine, other), jnp.where(here, other, mine)

    lefts = (grad_rows, hidden2)
    total0 = halves(lefts, (act_own, d_own), (act_oth, d_oth))
    share0 = reduce_rows(total0)

    oth1 = plane.pair(after(own1, act_own))
    own1, oth1 = fence(own1, oth1, total0)[:2]
    totals, sent, shared = {}, [], None
    for j in list(range(ranks - 1, 0, -1)) + [0]:
        totals[j], shared = feed_forward(
            j, turned[j], plane.block_places(), pieces[j], grad_rows, own1, oth1, half, size,
            sums[j], shared, BF if j else F32,
        )
        if j:
            sent.append(plane.swap(totals[j], j))
    act_own, act_oth, d_own, d_oth, *forth = shared
    total1 = halves(lefts, (act_own, d_own), (act_oth, d_oth))
    mine, *sent = fence(totals[0], *sent, total1)[:-1]
    dx1, da = back_chunk(grad_rows, resid1, mine, sent)
    share1 = reduce_rows(after(total1, da))

    da, dout = dmixed(plane.gather(da), wo_own, wo_oth, turned)
    dout, share0, *forth = fence(dout, share0, *forth)
    forth = plane.collect_blocks(forth)
    dquery, dkey, dvalue, edges = attend_back(
        query, key, value, halo, first, lse, dout, cos_tab, sin_tab
    )
    edges = lax.ppermute(edges, ("fsdp", "tp"), backward)
    da, *forth = fence(da, *forth, dquery)[:-1]
    others = [exchange(share) for share in fence(share0, share1, *forth)[:2]]
    total_out = halves(
        (da,), (mixed_rows[:, :head_cols],), (mixed_rows[:, head_cols:],)
    )
    share_out = reduce_rows(after(total_out, share0))
    edges = after(edges, total_out)
    d_own, d_oth = finish_attention(dquery, dkey, dvalue, edges)
    other_qkv = plane.pair(grads((hidden1,), (d_oth,)))
    layer_out = functools.reduce(jnp.add, [p.astype(F32) for p in forth]).astype(BF)
    other_qkv, layer_out, share_out, others[0] = fence(
        other_qkv, layer_out, share_out, others[0]
    )
    others.append(exchange(share_out))
    total_qkv = grads((hidden1,), (d_own,), other_qkv)
    share_qkv = reduce_rows(total_qkv)
    d_own, d_oth = fence(d_own, d_oth, total_qkv)[:2]
    parts = input_parts(
        plane.r, plane.block_places(), d_own, d_oth, qkv_own, qkv_oth, full_x, dx1
    )
    *parts, others[1], others[2] = fence(*parts, *others[1:])
    back = plane.collect_blocks(parts)

    done = [both_parts(share0, others[0]), both_parts(share1, others[1])]
    grad_down = jnp.concatenate([done[s][c][:, :half] for c in range(2) for s in range(2)], axis=1)
    grad_gate, grad_up = (
        jnp.concatenate(
            [
                done[s][c][:, half + (2 * n + which) * size : half + (2 * n + which + 1) * size]
                for c in range(2)
                for s in range(2)
                for n in range(half // size)
            ],
            axis=1,
        )
        for which in range(2)
    )
    grad_output = jnp.concatenate(both_parts(share_out, others[2]), axis=1)
    input_grad = functools.reduce(jnp.add, [p.astype(F32) for p in back]).astype(BF)
    qkv = both_parts(share_qkv, exchange(share_qkv))
    grad_query, grad_key, grad_value = (
        jnp.concatenate([p[:, i * head_cols : (i + 1) * head_cols] for p in qkv], axis=1)
        for i in range(3)
    )
    grads_out = (grad_query, grad_key, grad_value, grad_output, grad_gate, grad_up, grad_down)
    return (layer_out, input_grad) + tuple(g.astype(F32) for g in grads_out)


def solution(mesh):
    rows = P(("fsdp", "ctx"), "tp")
    weight = P("fsdp", "tp")
    return jax.shard_map(
        body,
        mesh=mesh,
        in_specs=(rows, rows, P(), P()) + (weight,) * 7,
        out_specs=(rows, rows) + (weight,) * 7,
        check_vma=False,
    )
```

```python
import functools
import math

import jax
import jax.numpy as jnp
from jax import lax
from jax.experimental import pallas as pl
from jax.experimental.pallas import tpu as pltpu
from jax.sharding import PartitionSpec as P

HD = 128
HALO = 1024
EPSILON = 1e-05
NEG_FILL = -1e30
PLANE = ("ctx", "tp")
BF = jnp.bfloat16
F32 = jnp.float32


def takes(microseconds):
    return pl.CostEstimate(
        flops=int(microseconds * 30e6), bytes_accessed=1, transcendentals=0
    )


def dot_plain(left, right):
    return jnp.dot(left, right, preferred_element_type=F32)


def dot_last(left, right):
    return lax.dot_general(left, right, (((1,), (1,)), ((), ())), preferred_element_type=F32)


def dot_rows(left, right):
    return lax.dot_general(left, right, (((0,), (0,)), ((), ())), preferred_element_type=F32)


def normalize(values):
    average = jnp.mean(values, axis=-1, keepdims=True)
    centred = values - average
    spread = jnp.mean(centred * centred, axis=-1, keepdims=True)
    inv_dev = lax.rsqrt(spread + EPSILON)
    return (centred * inv_dev, inv_dev)


def norm_back(grad, normed, inv_dev):
    grad_mean = jnp.mean(grad, axis=-1, keepdims=True)
    cross_mean = jnp.mean(grad * normed, axis=-1, keepdims=True)
    return inv_dev * (grad - grad_mean - normed * cross_mean)


def slots(lengths, order):
    seq_len = lengths.reshape(-1)
    seq_ids = jnp.arange(seq_len.shape[0], dtype=jnp.int32)
    picks = order[:, None] == seq_ids[None, :]
    order_len = jnp.sum(jnp.where(picks, seq_len[None, :], 0), axis=1)
    return jnp.cumsum(order_len) - order_len


def first_of(index, starts):
    inside = index[:, None] >= starts[None, :]
    return jnp.max(jnp.where(inside, starts[None, :], 0), axis=1)


def qkv_kernel(heads, table, *refs):
    *pieces, own_ref, oth_ref, cos_ref, sin_ref, x_ref, h_ref, q_ref, k_ref, v_ref, e_ref = refs
    cols = pieces[0].shape[1]
    for i, piece in enumerate(pieces):
        x_ref[:, pl.ds(pl.multiple_of(table[i] * cols, cols), cols)] = piece[...]
    values = x_ref[...].astype(F32)
    normed, _ = normalize(values)
    hidden = normed.astype(BF)
    h_ref[...] = hidden
    cos, sin = cos_ref[...], sin_ref[...]
    width = heads * HD
    for piece, w_ref in enumerate((own_ref, oth_ref)):
        out = dot_plain(hidden, w_ref[...])
        for head in range(heads):
            to = (piece * heads + head) * HD
            swapped = ((1 - piece) * heads + head) * HD
            query = out[:, head * HD : (head + 1) * HD]
            key = out[:, width + head * HD : width + (head + 1) * HD]
            value = out[:, 2 * width + head * HD : 2 * width + (head + 1) * HD].astype(BF)
            query = (query * cos + pltpu.roll(query, HD // 2, 1) * sin).astype(BF)
            key = (key * cos + pltpu.roll(key, HD // 2, 1) * sin).astype(BF)
            q_ref[:, to : to + HD] = query
            k_ref[:, to : to + HD] = key
            v_ref[:, to : to + HD] = value
            e_ref[:, swapped : swapped + HD] = key
            e_ref[:, 2 * width + swapped : 2 * width + swapped + HD] = value


def project(pieces, places, w_own, w_oth, cos_tab, sin_tab, heads):
    rows, cols = pieces[0].shape
    width = cols * len(pieces)
    block = rows // 3
    skip = rows // block - HALO // block
    local = 2 * heads * HD
    row = lambda i, t: (i, 0)
    once = pl.BlockSpec((width, 3 * heads * HD), lambda i, t: (0, 0))
    table = pl.BlockSpec((block, HD), lambda i, t: (i + HALO // block, 0))
    part = pl.BlockSpec((block, local), row)
    return pl.pallas_call(
        functools.partial(qkv_kernel, heads),
        grid_spec=pltpu.PrefetchScalarGridSpec(
            num_scalar_prefetch=1,
            grid=(rows // block,),
            in_specs=[pl.BlockSpec((block, cols), row)] * len(pieces) + [once, once, table, table],
            out_specs=[pl.BlockSpec((block, width), row)] * 2
            + [part] * 3
            + [pl.BlockSpec((block, 2 * local), lambda i, t: (jnp.maximum(i - skip, 0), 0))],
        ),
        out_shape=[jax.ShapeDtypeStruct((rows, width), BF)] * 2
        + [jax.ShapeDtypeStruct((rows, local), BF)] * 3
        + [jax.ShapeDtypeStruct((HALO, 2 * local), BF)],
        cost_estimate=takes(20),
        compiler_params=pltpu.CompilerParams(vmem_limit_bytes=60 << 20),
        name="norm_project",
    )(jnp.stack([jnp.asarray(p, jnp.int32) for p in places]), *pieces, w_own, w_oth, cos_tab, sin_tab)


def join_kernel(table, *refs):
    *pieces, out_ref = refs
    cols = pieces[0].shape[1]
    for i, piece in enumerate(pieces):
        out_ref[:, pl.ds(pl.multiple_of(table[i] * cols, cols), cols)] = piece[...]


def join(pieces, places, chunks):
    rows, cols = pieces[0].shape
    count, ranks = len(pieces), len(chunks)
    chunk = rows // ranks
    table = jnp.stack([jnp.asarray(v, jnp.int32) for v in list(places) + list(chunks)])
    piece = pl.BlockSpec((chunk, cols), lambda i, t: (t[count + i], 0))
    return pl.pallas_call(
        join_kernel,
        grid_spec=pltpu.PrefetchScalarGridSpec(
            num_scalar_prefetch=1,
            grid=(ranks,),
            in_specs=[piece] * count,
            out_specs=pl.BlockSpec((chunk, cols * count), lambda i, t: (i, 0)),
        ),
        out_shape=jax.ShapeDtypeStruct((rows, cols * count), pieces[0].dtype),
        cost_estimate=takes(5),
        compiler_params=pltpu.CompilerParams(vmem_limit_bytes=60 << 20),
        name="join",
    )(table, *pieces)


def pack_kernel(table, *refs):
    *ins, out_ref = refs
    at = 0
    for ref in ins:
        out_ref[:, at : at + ref.shape[1]] = ref[...]
        at += ref.shape[1]


def pack(weights, c, at, size, steps):
    rows = weights[0].shape[0]
    cols = weights[0].shape[1] // 2
    table = jnp.asarray(c, jnp.int32).reshape(1)
    spec = pl.BlockSpec((rows, size), lambda n, t: (0, t[0] * (cols // size) + at // size + n))
    return pl.pallas_call(
        pack_kernel,
        grid_spec=pltpu.PrefetchScalarGridSpec(
            num_scalar_prefetch=1,
            grid=(steps,),
            in_specs=[spec] * len(weights),
            out_specs=pl.BlockSpec((rows, size * len(weights)), lambda n, t: (0, n)),
        ),
        out_shape=jax.ShapeDtypeStruct((rows, size * len(weights) * steps), weights[0].dtype),
        cost_estimate=takes(2),
        compiler_params=pltpu.CompilerParams(vmem_limit_bytes=60 << 20),
        name="pack",
    )(table, *weights)


def allowed_keys(first_ref, step, block, span):
    keys = lax.broadcasted_iota(jnp.int32, (block, span), 1)
    rows = lax.broadcasted_iota(jnp.int32, (block, span), 0)
    skip = block + HALO - span
    first = first_ref[...] - (step * block + skip)
    return (keys >= first) & (keys <= rows + (HALO - skip))


def spans_of(first, block):
    steps = first.shape[0] // block
    lowest = jnp.min(first.reshape(steps, block), axis=1)
    own = jnp.arange(steps, dtype=jnp.int32) + HALO // block
    return own - lowest // block + 1


def by_span(need, block, body):
    for count in range(1, HALO // block + 2):
        pl.when(need == count)(functools.partial(body, count * block))


def attend_kernel(late, base, need, q_ref, k_ref, v_ref, *refs):
    if late:
        first_ref, o_ref, lse_ref = refs
    else:
        ke_ref, ve_ref, first_ref, _, _, o_ref, lse_ref, keys, values = refs
    step = pl.program_id(1) + base
    block = q_ref.shape[0]
    if late:
        keys, values = k_ref, v_ref
    else:

        @pl.when(pl.program_id(1) == 0)
        def _():
            keys[:HALO] = ke_ref[...]
            keys[HALO:] = k_ref[...]
            values[:HALO] = ve_ref[...]
            values[HALO:] = v_ref[...]

    def body(span):
        at = (step + 1) * block + (0 if late else HALO) - span
        window = pl.ds(pl.multiple_of(at, block), span)
        raw = dot_last(q_ref[...], keys[window, :]) * (HD**-0.5)
        raw = jnp.where(allowed_keys(first_ref, step, block, span), raw, NEG_FILL)
        top = jnp.max(raw, axis=-1, keepdims=True)
        expo = jnp.exp(raw - top)
        denom = jnp.sum(expo, axis=-1, keepdims=True)
        probs = (expo * (1.0 / denom)).astype(BF)
        o_ref[...] = dot_plain(probs, values[window, :]).astype(BF)
        lse_ref[...] = top + jnp.log(denom)

    by_span(need[step], block, body)


def attend(q, k, v, halo, first, done=None, block=256):
    rows, local = q.shape
    heads = local // HD
    late = halo is None
    base = HALO // block if late else 0
    steps = rows // block - base if late else HALO // block
    row = pl.BlockSpec((block, HD), lambda h, i, t: (base + i, h))
    column = pl.BlockSpec((rows, HD), lambda h, i, t: (0, h))
    bound = pl.BlockSpec((block, 1), lambda h, i, t: (base + i, 0))
    norm = pl.BlockSpec((None, block, 1), lambda h, i, t: (h, base + i, 0))
    if late:
        in_specs, operands, scratch, aliases = [row, column, column, bound], (q, k, v, first), [], {}
    else:
        edge = [pl.BlockSpec((HALO, HD), lambda h, i, t, at=at: (0, h + at)) for at in (0, heads)]
        whole = pl.BlockSpec(memory_space=pl.ANY)
        in_specs = [row, column, column] + edge + [bound, whole, whole]
        operands = (q, k, v, halo, halo, first) + tuple(done)
        scratch = [pltpu.VMEM((HALO + rows, HD), BF)] * 2
        aliases = {7: 0, 8: 1}
    return pl.pallas_call(
        functools.partial(attend_kernel, late, base),
        grid_spec=pltpu.PrefetchScalarGridSpec(
            num_scalar_prefetch=1,
            grid=(heads, steps),
            in_specs=in_specs,
            out_specs=[row, norm],
            scratch_shapes=scratch,
        ),
        out_shape=[
            jax.ShapeDtypeStruct((rows, local), BF),
            jax.ShapeDtypeStruct((heads, rows, 1), F32),
        ],
        input_output_aliases=aliases,
        cost_estimate=takes(10 if late else 20),
        compiler_params=pltpu.CompilerParams(vmem_limit_bytes=60 << 20),
        name="attend_late" if late else "attend_early",
    )(spans_of(first[:, 0], block), *operands)


def rotate_back(grad, cos, sin):
    return grad * cos - pltpu.roll(grad, HD // 2, 1) * sin


def attend_back_kernel(
    need, q_ref, k_ref, v_ref, ke_ref, ve_ref, first_ref, lse_ref, do_ref, cos_ref, sin_ref,
    dq_ref, dk_ref, dv_ref, e_ref, keys, values, dkeys, dvalues,
):
    step = pl.program_id(1)
    block = q_ref.shape[0]
    scale = HD**-0.5

    @pl.when(step == 0)
    def _():
        keys[:HALO] = ke_ref[...]
        keys[HALO:] = k_ref[...]
        values[:HALO] = ve_ref[...]
        values[HALO:] = v_ref[...]
        dkeys[...] = jnp.zeros_like(dkeys)
        dvalues[...] = jnp.zeros_like(dvalues)

    def body(span):
        window = pl.ds(pl.multiple_of((step + 1) * block + HALO - span, block), span)
        query, dout = q_ref[...], do_ref[...]
        raw = dot_last(query, keys[window, :]) * scale
        allowed = allowed_keys(first_ref, step, block, span)
        probs = jnp.where(allowed, jnp.exp(raw - lse_ref[...]), 0.0)
        dprob = dot_last(dout, values[window, :])
        delta = jnp.sum(probs * dprob, axis=-1, keepdims=True)
        dscore = (probs * (dprob - delta)).astype(BF)
        mine = pl.ds(pl.multiple_of(HALO + step * block, block), block)
        dquery = dot_plain(dscore, keys[window, :]) * scale
        dq_ref[...] = rotate_back(dquery, cos_ref[mine, :], sin_ref[mine, :]).astype(BF)
        dkeys[window, :] += dot_rows(dscore, query)
        dvalues[window, :] += dot_rows(probs.astype(BF), dout)

    by_span(need[step], block, body)

    @pl.when(step == pl.num_programs(1) - 1)
    def _():
        dkey = rotate_back(dkeys[...] * scale, cos_ref[...], sin_ref[...])
        e_ref[0] = dkey[:HALO].astype(BF)
        dk_ref[...] = dkey[HALO:]
        e_ref[1] = dvalues[:HALO].astype(BF)
        dv_ref[...] = dvalues[HALO:]


def attend_back(q, k, v, halo, first, lse, dout, cos_tab, sin_tab, block=256):
    rows, local = q.shape
    heads = local // HD
    span = block + HALO
    column = pl.BlockSpec((rows, HD), lambda h, i, t: (0, h))
    piece = pl.BlockSpec((block, HD), lambda h, i, t: (i, h))
    table = pl.BlockSpec((HALO + rows, HD), lambda h, i, t: (0, 0))
    edge = pl.BlockSpec((HALO, HD), lambda h, i, t: (0, h))
    return pl.pallas_call(
        attend_back_kernel,
        grid_spec=pltpu.PrefetchScalarGridSpec(
            num_scalar_prefetch=1,
            grid=(heads, rows // block),
            in_specs=[
                piece,
                column,
                column,
                edge,
                pl.BlockSpec((HALO, HD), lambda h, i, t: (0, h + heads)),
                pl.BlockSpec((block, 1), lambda h, i, t: (i, 0)),
                pl.BlockSpec((None, block, 1), lambda h, i, t: (h, i, 0)),
                piece,
                table,
                table,
            ],
            out_specs=[
                piece,
                column,
                column,
                pl.BlockSpec((2, HALO, HD), lambda h, i, t: (0, 0, (h + heads // 2) % heads)),
            ],
            scratch_shapes=[pltpu.VMEM((HALO + rows, HD), BF)] * 2
            + [pltpu.VMEM((HALO + rows, HD), F32)] * 2,
        ),
        out_shape=[
            jax.ShapeDtypeStruct((rows, local), BF),
            jax.ShapeDtypeStruct((rows, local), F32),
            jax.ShapeDtypeStruct((rows, local), F32),
            jax.ShapeDtypeStruct((2, HALO, local), BF),
        ],
        cost_estimate=takes(43),
        compiler_params=pltpu.CompilerParams(vmem_limit_bytes=60 << 20),
        name="attend_back",
    )(spans_of(first[:, 0], block), q, k, v, halo, halo, first, lse, dout, cos_tab, sin_tab)


def ffn_kernel(first_half, seeded, shared_count, steps, table, h_ref, g_ref, own_ref, oth_ref, *refs):
    count = 2 if not first_half else int(seeded)
    starts, refs = refs[:count], refs[count + shared_count :]
    back_ref, act_own, act_oth, d_own, d_oth, *refs = refs
    if first_half:
        forth_ref, keep_ref = refs
        back, forth = back_ref, forth_ref
    else:
        *outs, back, forth = refs
    step = pl.program_id(0)
    hidden, grad = h_ref[...], g_ref[...]
    size = own_ref.shape[1] // 3

    if first_half:

        @pl.when(step == 0)
        def _():
            keep_ref[...] = hidden

    for w_ref, act_ref, d_ref in ((own_ref, act_own, d_own), (oth_ref, act_oth, d_oth)):
        both = dot_plain(hidden, w_ref[:, : 2 * size])
        dact = dot_plain(grad, w_ref[:, 2 * size :]).astype(BF).astype(F32)
        gate, up = both[:, :size], both[:, size:]
        sig = jax.nn.sigmoid(gate)
        silu = gate * sig
        act_ref[...] = (silu * up).astype(BF)
        d_ref[:, :size] = (dact * up * sig * (1.0 + gate * (1.0 - sig))).astype(BF)
        d_ref[:, size:] = (dact * silu).astype(BF)

    def add(first, last):
        tile = back_ref.shape[1] // 4
        for at in range(0, 4 * tile, tile):
            cols = slice(at, at + tile)
            more = dot_last(act_own[...], own_ref[cols, 2 * size :])
            more += dot_last(act_oth[...], oth_ref[cols, 2 * size :])
            grad = dot_last(d_own[...], own_ref[cols, : 2 * size])
            grad += dot_last(d_oth[...], oth_ref[cols, : 2 * size])
            if not first:
                more += forth[:, cols]
                grad += back[:, cols]
            elif not first_half:
                more += starts[1][:, cols]
                grad += starts[0][:, cols]
            elif seeded:
                more += starts[0][:, cols]
            if first_half or not last:
                forth[:, cols] = more
                back[:, cols] = grad
                continue
            back_ref[:, cols] = grad.astype(back_ref.dtype)
            if steps == 1 or len(outs) != 4:
                forth[:, cols] = more
                continue
            for i, out_ref in enumerate(outs):

                @pl.when(table[1 + i] == at // tile)
                def _():
                    out_ref[...] = more.astype(BF)

        if last and not first_half and (steps == 1 or len(outs) != 4):
            for i, out_ref in enumerate(outs):
                cols = out_ref.shape[1]
                at = pl.multiple_of(table[1 + i] * cols, cols)
                out_ref[...] = forth[:, pl.ds(at, cols)].astype(BF)

    if steps == 1:
        add(True, True)
    else:
        pl.when(step == 0)(lambda: add(True, False))
        if steps > 2:
            pl.when((step > 0) & (step < steps - 1))(lambda: add(False, False))
        pl.when(step == steps - 1)(lambda: add(False, True))


def feed_forward(j, place, places, hidden, grad_rows, w_own, w_oth, half, size, starts, shared, kind):
    chunk, width = hidden.shape
    rows = grad_rows.shape[0]
    first_half = places is None
    steps = half // size
    fixed = pl.BlockSpec((chunk, width), lambda n, t: (0, 0))
    at_j = pl.BlockSpec((chunk, width), lambda n, t: (j, 0))
    weight = pl.BlockSpec((width, 3 * size), lambda n, t: (0, n))
    table = jnp.stack([jnp.asarray(p, jnp.int32) for p in [place] + list(places or [])])
    starts = [] if starts is None else list(starts)
    operands = [hidden, grad_rows, w_own, w_oth] + starts
    in_specs = [fixed, at_j, weight, weight] + [fixed] * len(starts)
    act = pl.BlockSpec((chunk, size), lambda n, t: (j, n))
    both = pl.BlockSpec((chunk, 2 * size), lambda n, t: (j, n))
    out_specs = [fixed, act, act, both, both]
    out_shape = (
        [jax.ShapeDtypeStruct((chunk, width), kind)]
        + [jax.ShapeDtypeStruct((rows, half), BF)] * 2
        + [jax.ShapeDtypeStruct((rows, 2 * half), BF)] * 2
    )
    shared_at = [1, 2, 3, 4]
    if first_half:
        out_specs += [fixed, at_j]
        out_shape += [
            jax.ShapeDtypeStruct((chunk, width), F32),
            jax.ShapeDtypeStruct((rows, width), BF),
        ]
        shared_at.append(6)
    else:
        cols = width // len(places)
        out_specs += [pl.BlockSpec((chunk, cols), lambda n, t: (t[0], 0))] * len(places)
        out_shape += [jax.ShapeDtypeStruct((rows, cols), BF)] * len(places)
        shared_at += [5 + i for i in range(len(places))]
    aliases = {}
    if shared is not None:
        aliases = {1 + len(operands) + i: at for i, at in enumerate(shared_at)}
        in_specs += [pl.BlockSpec(memory_space=pl.ANY)] * len(shared)
        operands += list(shared)
    out = pl.pallas_call(
        functools.partial(
            ffn_kernel, first_half, len(starts) == 1, 0 if shared is None else len(shared), steps
        ),
        grid_spec=pltpu.PrefetchScalarGridSpec(
            num_scalar_prefetch=1,
            grid=(steps,),
            in_specs=in_specs,
            out_specs=out_specs,
            scratch_shapes=[] if first_half else [pltpu.VMEM((chunk, width), F32)] * 2,
        ),
        out_shape=out_shape,
        input_output_aliases=aliases,
        cost_estimate=takes(20),
        compiler_params=pltpu.CompilerParams(vmem_limit_bytes=60 << 20),
        name="feed_forward",
    )(table, *operands)
    sums = [out[0], out[5]] if first_half else out[0]
    return sums, [out[at] for at in shared_at]


def finish_kernel(dq, dk, dv, e_ref, d_own, d_oth, edges):
    step = pl.program_id(0)
    chunk, local = dq.shape
    lead = edges.shape[1] - e_ref.shape[1]

    @pl.when(step == 0)
    def _():
        edges[:, :lead] = jnp.zeros((2, lead, local), BF)
        edges[:, lead:] = e_ref[...]

    rows = pl.ds(pl.multiple_of(step * chunk, chunk), chunk)
    dkey = (dk[...] + edges[0, rows, :].astype(F32)).astype(BF)
    dvalue = (dv[...] + edges[1, rows, :].astype(F32)).astype(BF)
    cols = local // 2
    for ref, at in ((d_own, 0), (d_oth, cols)):
        ref[:, :cols] = dq[:, at : at + cols]
        ref[:, cols : 2 * cols] = dkey[:, at : at + cols]
        ref[:, 2 * cols :] = dvalue[:, at : at + cols]


def finish_attention(dq, dk, dv, edges, block=256):
    rows, local = dq.shape
    inner = 3 * local // 2
    row = lambda i: (i, 0)
    part = pl.BlockSpec((block, local), row)
    return pl.pallas_call(
        finish_kernel,
        grid=(rows // block,),
        in_specs=[part, part, part, pl.BlockSpec(edges.shape, lambda i: (0, 0, 0))],
        out_specs=[pl.BlockSpec((block, inner), row)] * 2,
        out_shape=[jax.ShapeDtypeStruct((rows, inner), BF)] * 2,
        scratch_shapes=[pltpu.VMEM((2, rows, local), BF)],
        cost_estimate=takes(4),
        compiler_params=pltpu.CompilerParams(vmem_limit_bytes=60 << 20),
        name="finish_attention",
    )(dq, dk, dv, edges)


def input_kernel(table, d_own, d_oth, w_own, w_oth, x_ref, dx_ref, *outs):
    step = pl.program_id(0)
    grad = dot_last(d_own[...], w_own[...]) + dot_last(d_oth[...], w_oth[...])
    normed, inv_dev = normalize(x_ref[...].astype(F32))
    grad = norm_back(grad, normed, inv_dev)
    keep = jnp.where(step == table[0], 1.0, 0.0)
    grad = (grad + keep * dx_ref[...]).astype(BF)
    for i, out_ref in enumerate(outs):
        width = out_ref.shape[1]
        for t in range(len(outs)):

            @pl.when(table[1 + i] == t)
            def _():
                out_ref[...] = grad[:, t * width : (t + 1) * width]


def input_parts(rank, places, d_own, d_oth, w_own, w_oth, full_x, dx1):
    rows, width = full_x.shape
    chunk = dx1.shape[0]
    inner = w_own.shape[1]
    cols = width // len(places)
    row = lambda i, t: (i, 0)
    once = lambda i, t: (0, 0)
    return pl.pallas_call(
        input_kernel,
        grid_spec=pltpu.PrefetchScalarGridSpec(
            num_scalar_prefetch=1,
            grid=(rows // chunk,),
            in_specs=[
                pl.BlockSpec((chunk, inner), row),
                pl.BlockSpec((chunk, inner), row),
                pl.BlockSpec((width, inner), once),
                pl.BlockSpec((width, inner), once),
                pl.BlockSpec((chunk, width), row),
                pl.BlockSpec((chunk, width), once),
            ],
            out_specs=[pl.BlockSpec((chunk, cols), row)] * len(places),
        ),
        out_shape=[jax.ShapeDtypeStruct((rows, cols), BF)] * len(places),
        cost_estimate=takes(20),
        compiler_params=pltpu.CompilerParams(vmem_limit_bytes=60 << 20),
        name="input_parts",
    )(
        jnp.stack([jnp.asarray(p, jnp.int32) for p in [rank] + list(places)]),
        d_own, d_oth, w_own, w_oth, full_x, dx1,
    )


def shares_kernel(table, m_ref, w_own, w_oth, keep_ref, mine_ref, *refs):
    cols = w_own.shape[1]
    keep_ref[...] = m_ref[...]
    out = dot_last(m_ref[:, :cols], w_own[...]) + dot_last(m_ref[:, cols:], w_oth[...])
    for j, ref in enumerate((mine_ref,) + refs):

        @pl.when(pl.program_id(0) == j)
        def _():
            ref[...] = out.astype(ref.dtype)


def output_shares(mixed, w_own, w_oth, turned):
    rows, local = mixed.shape
    width, cols = w_own.shape
    ranks = len(turned)
    chunk = rows // ranks
    once = lambda j, t: (0, 0)
    return pl.pallas_call(
        shares_kernel,
        grid_spec=pltpu.PrefetchScalarGridSpec(
            num_scalar_prefetch=1,
            grid=(ranks,),
            in_specs=[
                pl.BlockSpec((chunk, local), lambda j, t: (t[j], 0)),
                pl.BlockSpec((width, cols), once),
                pl.BlockSpec((width, cols), once),
            ],
            out_specs=[pl.BlockSpec((chunk, local), lambda j, t: (j, 0))]
            + [pl.BlockSpec((chunk, width), once)] * ranks,
        ),
        out_shape=[
            jax.ShapeDtypeStruct((rows, local), BF),
            jax.ShapeDtypeStruct((chunk, width), F32),
        ]
        + [jax.ShapeDtypeStruct((chunk, width), BF)] * (ranks - 1),
        cost_estimate=takes(7),
        compiler_params=pltpu.CompilerParams(vmem_limit_bytes=60 << 20),
        name="output_shares",
    )(jnp.stack(turned).astype(jnp.int32), mixed, w_own, w_oth)


def dmixed_kernel(table, *refs):
    *chunks, w_own, w_oth, keep_ref, d_ref = refs
    cols = w_own.shape[1]
    for j in range(len(chunks)):

        @pl.when(pl.program_id(0) == j)
        def _():
            chunk = chunks[j][...]
            keep_ref[...] = chunk
            d_ref[:, :cols] = dot_plain(chunk, w_own[...]).astype(BF)
            d_ref[:, cols:] = dot_plain(chunk, w_oth[...]).astype(BF)


def dmixed(chunks, w_own, w_oth, turned):
    chunk, width = chunks[0].shape
    cols = w_own.shape[1]
    ranks = len(chunks)
    once = lambda j, t: (0, 0)
    return pl.pallas_call(
        dmixed_kernel,
        grid_spec=pltpu.PrefetchScalarGridSpec(
            num_scalar_prefetch=1,
            grid=(ranks,),
            in_specs=[pl.BlockSpec((chunk, width), once)] * ranks
            + [pl.BlockSpec((width, cols), once)] * 2,
            out_specs=[
                pl.BlockSpec((chunk, width), lambda j, t: (j, 0)),
                pl.BlockSpec((chunk, 2 * cols), lambda j, t: (t[j], 0)),
            ],
        ),
        out_shape=[
            jax.ShapeDtypeStruct((chunk * ranks, width), BF),
            jax.ShapeDtypeStruct((chunk * ranks, 2 * cols), BF),
        ],
        cost_estimate=takes(7),
        compiler_params=pltpu.CompilerParams(vmem_limit_bytes=60 << 20),
        name="dmixed",
    )(jnp.stack(turned).astype(jnp.int32), *chunks, w_own, w_oth)


def norm_kernel(table, x_ref, mine_ref, *refs):
    *others, resid_ref, h_ref = refs
    total = x_ref[...].astype(F32) + mine_ref[...]
    for ref in others:
        total = total + ref[...].astype(F32)
    resid_ref[...] = total
    h_ref[...] = normalize(total)[0].astype(BF)


def norm_chunk(rank, full_x, mine, others):
    chunk, width = mine.shape
    block = chunk // 3
    row = pl.BlockSpec((block, width), lambda i, t: (i, 0))
    return pl.pallas_call(
        norm_kernel,
        grid_spec=pltpu.PrefetchScalarGridSpec(
            num_scalar_prefetch=1,
            grid=(3,),
            in_specs=[pl.BlockSpec((block, width), lambda i, t: (t[0] * 3 + i, 0)), row]
            + [row] * len(others),
            out_specs=[row, row],
        ),
        out_shape=[
            jax.ShapeDtypeStruct((chunk, width), F32),
            jax.ShapeDtypeStruct((chunk, width), BF),
        ],
        cost_estimate=takes(4),
        compiler_params=pltpu.CompilerParams(vmem_limit_bytes=60 << 20),
        name="norm_chunk",
    )(jnp.asarray(rank, jnp.int32).reshape(1), full_x, mine, *others)


def back_kernel(g_ref, resid_ref, mine_ref, *refs):
    *others, dx_ref, da_ref = refs
    total = mine_ref[...]
    for ref in others:
        total = total + ref[...].astype(F32)
    normed, inv_dev = normalize(resid_ref[...])
    dx = g_ref[...].astype(F32) + norm_back(total, normed, inv_dev)
    dx_ref[...] = dx
    da_ref[...] = dx.astype(BF)


def back_chunk(grad_rows, resid1, mine, others):
    chunk, width = mine.shape
    block = chunk // 3
    row = pl.BlockSpec((block, width), lambda i: (i, 0))
    return pl.pallas_call(
        back_kernel,
        grid=(3,),
        in_specs=[row] * (3 + len(others)),
        out_specs=[row, row],
        out_shape=[
            jax.ShapeDtypeStruct((chunk, width), F32),
            jax.ShapeDtypeStruct((chunk, width), BF),
        ],
        cost_estimate=takes(4),
        compiler_params=pltpu.CompilerParams(vmem_limit_bytes=60 << 20),
        name="back_chunk",
    )(grad_rows, resid1, mine, *others)


def grads_kernel(count, *refs):
    *ins, out_ref = refs
    at = 0
    for left, right in zip(ins[:count], ins[count : 2 * count]):
        cols = right.shape[1]
        total = dot_rows(left[...], right[...])
        if len(ins) > 2 * count:
            total = total + ins[-1][:, at : at + cols].astype(F32)
        out_ref[:, at : at + cols] = total.astype(BF)
        at += cols


def grads(lefts, rights, other=None):
    rows, width = lefts[0].shape
    cols = sum(r.shape[1] for r in rights)
    block = 512
    in_specs = [pl.BlockSpec((rows, block), lambda m: (0, m))] * len(lefts)
    in_specs += [pl.BlockSpec(r.shape, lambda m: (0, 0)) for r in rights]
    out = pl.BlockSpec((block, cols), lambda m: (m, 0))
    operands = list(lefts) + list(rights)
    if other is not None:
        in_specs.append(out)
        operands.append(other)
    return pl.pallas_call(
        functools.partial(grads_kernel, len(lefts)),
        grid=(width // block,),
        in_specs=in_specs,
        out_specs=out,
        out_shape=jax.ShapeDtypeStruct((width, cols), BF),
        cost_estimate=takes(10),
        compiler_params=pltpu.CompilerParams(vmem_limit_bytes=60 << 20),
        name="grads",
    )(*operands)


def after(value, *others):
    return lax.optimization_barrier((value,) + others)[0]


class Plane:
    def __init__(self):
        self.nc, self.nt = lax.axis_size("ctx"), lax.axis_size("tp")
        assert self.nc == 2 and self.nt % 2 == 0
        self.hi = self.nt // self.nc
        self.ranks = self.nc * self.hi
        tp_place = lax.axis_index("tp")
        self.c = lax.axis_index("ctx")
        self.h, self.k = tp_place // self.nc, tp_place % self.nc
        self.r = self.c * self.hi + self.h

    def perm(self, move):
        pairs = []
        for c in range(self.nc):
            for h in range(self.hi):
                for k in range(self.nc):
                    c2, h2, k2 = move(c, h, k)
                    pairs.append((c * self.nt + h * self.nc + k, c2 * self.nt + h2 * self.nc + k2))
        return pairs

    def spread_rows(self, block):
        got = []
        for jh in range(self.hi):
            for jk in range(self.nc):
                move = lambda c, h, k: (k ^ jk, h ^ jh, c)
                place = (self.h ^ jh) * self.nc + (self.c ^ jk)
                got.append((place, lax.ppermute(block, PLANE, self.perm(move))))
        return got

    def spread_own(self, block, jh=0):
        got = []
        for jk in range(self.nc):
            move = lambda c, h, k: (k ^ jk, h, c)
            place = (self.h ^ jh) * self.nc + (self.c ^ jk)
            got.append((place, lax.ppermute(block, PLANE, self.perm(move))))
        return got

    def turn_pairs(self, block, jh):
        return lax.ppermute(block, PLANE, self.perm(lambda c, h, k: (c, h ^ jh, k)))

    def block_places(self):
        return [
            (self.h ^ jh) * self.nc + (self.c ^ jk) for jh in range(self.hi) for jk in range(self.nc)
        ]

    def collect_blocks(self, pieces):
        moves = [
            lambda c, h, k, jh=jh, jk=jk: (k, h ^ jh, c ^ jk)
            for jh in range(self.hi)
            for jk in range(self.nc)
        ]
        return [lax.ppermute(p, PLANE, self.perm(m)) for p, m in zip(pieces, moves)]

    def sum_pairs(self, pieces):
        sent = [
            lax.ppermute(
                pieces[jh * self.nc + jk],
                PLANE,
                self.perm(lambda c, h, k, jh=jh: (c, h ^ jh, k)),
            )
            for jh in range(1, self.hi)
            for jk in range(self.nc)
        ]
        return [sent[jk :: self.nc] for jk in range(self.nc)]

    def sum_blocks(self, own):
        return [
            lax.ppermute(own[jk], PLANE, self.perm(lambda c, h, k, jk=jk: (k, h, c ^ jk)))
            for jk in range(self.nc)
        ]

    def swap(self, value, j):
        def move(c, h, k):
            rank = (c * self.hi + h) ^ j
            return rank // self.hi, rank % self.hi, k

        return lax.ppermute(value, PLANE, self.perm(move))

    def chunk_of(self, value, j):
        size = value.shape[0] // self.ranks
        return lax.dynamic_slice_in_dim(value, (self.r ^ j) * size, size, 0)

    def turn(self, value):
        return jnp.concatenate([self.chunk_of(value, j) for j in range(self.ranks)], axis=0)

    def gather(self, mine, use=None):
        use = use or (lambda j, chunk: chunk[:8, :128])
        out = [mine]
        if self.ranks != 4:
            out += [self.swap(mine, j) for j in range(1, self.ranks)]
            for j in range(self.ranks):
                use(j, out[j])
            return out
        near, far = self.swap(mine, 1), self.swap(mine, 2)
        near, far, _ = lax.optimization_barrier((near, far, use(0, mine)))
        half = mine.shape[0] // 2
        corner = [self.swap(near[:half], 2), self.swap(far[half:], 1)]
        use(1, near)
        last = use(2, far)
        corner = jnp.concatenate(lax.optimization_barrier((*corner, last))[:2], axis=0)
        use(3, corner)
        return [mine, near, far, corner]

    def pair(self, value):
        perm = [(t, t ^ 1) for t in range(self.nt)]
        return lax.ppermute(value, "tp", perm)


def body(
    tokens, cotangent, lengths, order, w_query, w_key, w_value, w_output, w_gate, w_up, w_down
):
    plane = Plane()
    rows = tokens.shape[0]
    nf, nc, nt, ranks = lax.axis_size("fsdp"), plane.nc, plane.nt, plane.ranks
    z = lax.axis_index("fsdp")
    chunk = rows // ranks
    head_cols = w_query.shape[1] // nc
    heads = head_cols // HD
    hidden_cols = w_gate.shape[1] // nc
    half = hidden_cols // 2
    size = min(256, half)

    def over_fsdp(shard):
        return lax.all_gather(shard, "fsdp", axis=0, tiled=True)

    fence = lambda *values: lax.optimization_barrier(values)
    turned = [plane.r ^ j for j in range(ranks)]

    qkv_own = over_fsdp(pack((w_query, w_key, w_value), plane.c, 0, head_cols, 1))
    places, got_x = zip(*plane.spread_rows(tokens))
    base = (z * nc + plane.k) * rows - HALO
    index = base + jnp.arange(HALO + rows, dtype=jnp.int32)
    starts = first_of(index, slots(lengths, order))
    within = index - starts
    first = (starts[HALO:] - base)[:, None]
    lane = jnp.arange(HD, dtype=jnp.int32)
    freq = jnp.exp((lane % (HD // 2)).astype(F32) * (-2.0 * math.log(10000.0) / HD))
    angle = within.astype(F32)[:, None] * freq[None, :]
    cos_tab = jnp.cos(angle)
    sin_tab = jnp.sin(angle) * jnp.where(lane < HD // 2, -1.0, 1.0)[None, :]
    qkv_own, cos_tab, sin_tab, first, *got_x = fence(qkv_own, cos_tab, sin_tab, first, *got_x)
    qkv_oth = plane.pair(qkv_own)
    w_output, cotangent = fence(w_output, cotangent, *got_x)[:2]
    wo_own = over_fsdp(pack((w_output,), plane.c, 0, head_cols, 1))
    own_g = plane.spread_own(cotangent)
    far_g = [plane.turn_pairs(cotangent, jh) for jh in range(1, plane.hi)]
    places_g = [place for place, _ in own_g]

    full_x, hidden1, query, key, value, edge = project(
        got_x, places, qkv_own, qkv_oth, cos_tab, sin_tab, heads
    )
    onward = []
    for f in range(nf):
        for h in range(plane.hi):
            for k in range(nc):
                to = f * nc + k + 1
                if to < nf * nc:
                    onward.append((f * nt + h * nc + k, to // nc * nt + h * nc + to % nc))
    backward = [(b, a) for a, b in onward]
    halo = lax.ppermute(edge, ("fsdp", "tp"), onward)
    wo_oth = plane.pair(after(wo_own, edge))
    late = attend(query, key, value, None, first)
    late, far_g, own_g = fence(late, far_g, [piece for _, piece in own_g])
    got_g = []
    for jh in range(1, plane.hi):
        for place, piece in plane.spread_own(far_g[jh - 1], jh):
            places_g.append(place)
            got_g.append(piece)
    halo, wo_own, wo_oth, *late = fence(halo, wo_own, wo_oth, *late)
    shard0 = pack(after((w_gate, w_up, w_down), halo), plane.c, 0, size, half // size)
    own0 = over_fsdp(shard0)
    mixed, lse = attend(query, key, value, after(halo, shard0), first, late)
    early = len(got_g) // 2
    mixed, got_g[:early] = fence(mixed, got_g[:early])

    mixed_rows, mine, *shares = output_shares(mixed, wo_own, wo_oth, turned)
    sent = [plane.swap(shares[j - 1], j) for j in range(ranks - 1, 0, -1)]
    mine, *got_g = fence(mine, *own_g, *got_g)
    grad_rows = join(got_g, places_g, turned)
    shard1 = pack(after((w_gate, w_up, w_down), mine), plane.c, half, size, half // size)
    own1 = over_fsdp(shard1)
    mine, grad_rows, *sent = fence(mine, grad_rows, *sent, shard1)[:-1]
    oth0 = plane.pair(after(own0, sent[0]))
    resid1, mine = norm_chunk(plane.r, full_x, mine, sent)

    sums, shared = {}, None

    def first_half(j, piece):
        nonlocal shared
        sums[j], shared = feed_forward(
            j, turned[j], None, piece, grad_rows, own0, oth0, half, size,
            None if j else [resid1], shared, F32,
        )
        return sums[j][0]

    pieces = plane.gather(mine, first_half)
    act_own, act_oth, d_own, d_oth, hidden2 = shared

    def halves(lefts, rights_own, rights_oth):
        return grads(lefts, rights_own, plane.pair(grads(lefts, rights_oth)))

    def reduce_rows(total):
        return lax.psum_scatter(total, "fsdp", scatter_dimension=0, tiled=True)

    def exchange(mine):
        return lax.ppermute(mine, "ctx", [(0, 1), (1, 0)])

    def both_parts(mine, other):
        here = plane.c == 0
        return jnp.where(here, mine, other), jnp.where(here, other, mine)

    lefts = (grad_rows, hidden2)
    total0 = halves(lefts, (act_own, d_own), (act_oth, d_oth))
    share0 = reduce_rows(total0)

    oth1 = plane.pair(after(own1, act_own))
    own1, oth1 = fence(own1, oth1, total0)[:2]
    totals, sent, shared = {}, [], None
    for at, j in enumerate(list(range(ranks - 1, 0, -1)) + [0]):
        piece = pieces[j]
        if at > 2:
            piece, sent[at - 3] = fence(piece, sent[at - 3])
        totals[j], shared = feed_forward(
            j, turned[j], plane.block_places(), piece, grad_rows, own1, oth1, half, size,
            sums[j], shared, BF if j else F32,
        )
        if j:
            sent.append(plane.swap(totals[j], j))
    act_own, act_oth, d_own, d_oth, *forth = shared
    act_oth, *sent[:-1] = fence(act_oth, *sent[:-1])
    other1 = grads(lefts, (act_oth, d_oth))
    mine, sent[-1], other1 = fence(totals[0], sent[-1], other1)
    other1 = plane.pair(other1)
    dx1, da = back_chunk(grad_rows, resid1, mine, sent)

    def own_grads(j, _):
        nonlocal total1
        if total1 is None:
            total1 = grads(lefts, fence(act_own, d_own, da)[:2], other1)
        return total1

    total1 = None
    da_pieces = plane.gather(da, own_grads)
    share1 = reduce_rows(fence(total1, *da_pieces[1:3])[0])

    da, dout = dmixed(da_pieces, wo_own, wo_oth, turned)
    dout, share0, *forth = fence(dout, share0, *forth)
    others = [exchange(share0)]
    pairs = plane.sum_pairs(forth)
    dquery, dkey, dvalue, edges = attend_back(
        query, key, value, halo, first, lse, dout, cos_tab, sin_tab
    )
    edges = lax.ppermute(edges, ("fsdp", "tp"), backward)
    dquery, pairs, others[0] = fence(dquery, pairs, others[0])
    own = [
        functools.reduce(jnp.add, [p.astype(F32) for p in [forth[jk]] + pairs[jk]]).astype(BF)
        for jk in range(nc)
    ]
    forth = plane.sum_blocks(own)
    da, mixed_rows = fence(da, mixed_rows, *own)[:2]
    total_out = halves((da,), (mixed_rows[:, :head_cols],), (mixed_rows[:, head_cols:],))
    share_out = reduce_rows(total_out)
    edges = after(edges, total_out)
    others.append(exchange(after(share1, *forth)))
    d_own, d_oth = finish_attention(dquery, dkey, dvalue, edges)
    other2 = grads((hidden1,), (d_oth,))
    other2, *forth = fence(other2, *forth)
    other2 = plane.pair(other2)
    layer_out = functools.reduce(jnp.add, [p.astype(F32) for p in forth]).astype(BF)
    other2, layer_out = fence(other2, layer_out)
    total2 = grads((hidden1,), (d_own,), other2)
    share2 = reduce_rows(total2)
    d_own, d_oth = fence(d_own, d_oth, total2)[:2]
    parts = input_parts(
        plane.r, plane.block_places(), d_own, d_oth, qkv_own, qkv_oth, full_x, dx1
    )
    *parts, others[1] = fence(*parts, others[1])
    back = plane.collect_blocks(parts)

    done = [both_parts(share0, others[0]), both_parts(share1, others[1])]
    grad_down = jnp.concatenate([done[s][c][:, :half] for c in range(2) for s in range(2)], axis=1)
    grad_gate, grad_up = (
        jnp.concatenate(
            [
                done[s][c][:, half + (2 * n + which) * size : half + (2 * n + which + 1) * size]
                for c in range(2)
                for s in range(2)
                for n in range(half // size)
            ],
            axis=1,
        )
        for which in range(2)
    )
    other2 = exchange(share2)
    back, other2, share2 = fence(back, other2, share2)
    last = both_parts(share2, other2)
    grad_query, grad_key, grad_value = (
        jnp.concatenate([p[:, i * head_cols : (i + 1) * head_cols] for p in last], axis=1)
        for i in range(3)
    )
    grad_output = jnp.concatenate(
        both_parts(share_out, exchange(after(share_out, back[0]))), axis=1
    )
    input_grad = functools.reduce(jnp.add, [p.astype(F32) for p in back]).astype(BF)
    grads_out = (grad_query, grad_key, grad_value, grad_output, grad_gate, grad_up, grad_down)
    return (layer_out, input_grad) + tuple(g.astype(F32) for g in grads_out)


def solution(mesh):
    rows = P(("fsdp", "ctx"), "tp")
    weight = P("fsdp", "tp")
    return jax.shard_map(
        body,
        mesh=mesh,
        in_specs=(rows, rows, P(), P()) + (weight,) * 7,
        out_specs=(rows, rows) + (weight,) * 7,
        check_vma=False,
    )
```

```python
import functools
import math

import jax
import jax.numpy as jnp
from jax import lax
from jax.experimental import pallas as pl
from jax.experimental.pallas import tpu as pltpu
from jax.sharding import PartitionSpec as P

HD = 128
HALO = 1024
EPSILON = 1e-05
NEG_FILL = -1e30
PLANE = ("ctx", "tp")
BF = jnp.bfloat16
F32 = jnp.float32


def takes(microseconds):
    return pl.CostEstimate(
        flops=int(microseconds * 30e6), bytes_accessed=1, transcendentals=0
    )


def dot_plain(left, right):
    return jnp.dot(left, right, preferred_element_type=F32)


def dot_last(left, right):
    return lax.dot_general(left, right, (((1,), (1,)), ((), ())), preferred_element_type=F32)


def dot_rows(left, right):
    return lax.dot_general(left, right, (((0,), (0,)), ((), ())), preferred_element_type=F32)


def normalize(values):
    average = jnp.mean(values, axis=-1, keepdims=True)
    centred = values - average
    spread = jnp.mean(centred * centred, axis=-1, keepdims=True)
    inv_dev = lax.rsqrt(spread + EPSILON)
    return (centred * inv_dev, inv_dev)


def norm_back(grad, normed, inv_dev):
    grad_mean = jnp.mean(grad, axis=-1, keepdims=True)
    cross_mean = jnp.mean(grad * normed, axis=-1, keepdims=True)
    return inv_dev * (grad - grad_mean - normed * cross_mean)


def slots(lengths, order):
    seq_len = lengths.reshape(-1)
    seq_ids = jnp.arange(seq_len.shape[0], dtype=jnp.int32)
    picks = order[:, None] == seq_ids[None, :]
    order_len = jnp.sum(jnp.where(picks, seq_len[None, :], 0), axis=1)
    return jnp.cumsum(order_len) - order_len


def first_of(index, starts):
    inside = index[:, None] >= starts[None, :]
    return jnp.max(jnp.where(inside, starts[None, :], 0), axis=1)


def qkv_kernel(heads, table, *refs):
    *pieces, own_ref, oth_ref, cos_ref, sin_ref, x_ref, h_ref, q_ref, k_ref, v_ref, e_ref = refs
    cols = pieces[0].shape[1]
    for i, piece in enumerate(pieces):
        x_ref[:, pl.ds(pl.multiple_of(table[i] * cols, cols), cols)] = piece[...]
    values = x_ref[...].astype(F32)
    normed, _ = normalize(values)
    hidden = normed.astype(BF)
    h_ref[...] = hidden
    cos, sin = cos_ref[...], sin_ref[...]
    width = heads * HD
    for piece, w_ref in enumerate((own_ref, oth_ref)):
        out = dot_plain(hidden, w_ref[...])
        for head in range(heads):
            to = (piece * heads + head) * HD
            swapped = ((1 - piece) * heads + head) * HD
            query = out[:, head * HD : (head + 1) * HD]
            key = out[:, width + head * HD : width + (head + 1) * HD]
            value = out[:, 2 * width + head * HD : 2 * width + (head + 1) * HD].astype(BF)
            query = (query * cos + pltpu.roll(query, HD // 2, 1) * sin).astype(BF)
            key = (key * cos + pltpu.roll(key, HD // 2, 1) * sin).astype(BF)
            q_ref[:, to : to + HD] = query
            k_ref[:, to : to + HD] = key
            v_ref[:, to : to + HD] = value
            e_ref[:, swapped : swapped + HD] = key
            e_ref[:, 2 * width + swapped : 2 * width + swapped + HD] = value


def project(pieces, places, w_own, w_oth, cos_tab, sin_tab, heads):
    rows, cols = pieces[0].shape
    width = cols * len(pieces)
    block = rows // 3
    skip = rows // block - HALO // block
    local = 2 * heads * HD
    row = lambda i, t: (i, 0)
    once = pl.BlockSpec((width, 3 * heads * HD), lambda i, t: (0, 0))
    table = pl.BlockSpec((block, HD), lambda i, t: (i + HALO // block, 0))
    part = pl.BlockSpec((block, local), row)
    return pl.pallas_call(
        functools.partial(qkv_kernel, heads),
        grid_spec=pltpu.PrefetchScalarGridSpec(
            num_scalar_prefetch=1,
            grid=(rows // block,),
            in_specs=[pl.BlockSpec((block, cols), row)] * len(pieces) + [once, once, table, table],
            out_specs=[pl.BlockSpec((block, width), row)] * 2
            + [part] * 3
            + [pl.BlockSpec((block, 2 * local), lambda i, t: (jnp.maximum(i - skip, 0), 0))],
        ),
        out_shape=[jax.ShapeDtypeStruct((rows, width), BF)] * 2
        + [jax.ShapeDtypeStruct((rows, local), BF)] * 3
        + [jax.ShapeDtypeStruct((HALO, 2 * local), BF)],
        cost_estimate=takes(20),
        compiler_params=pltpu.CompilerParams(vmem_limit_bytes=60 << 20),
        name="norm_project",
    )(jnp.stack([jnp.asarray(p, jnp.int32) for p in places]), *pieces, w_own, w_oth, cos_tab, sin_tab)


def join_kernel(table, *refs):
    *pieces, out_ref = refs
    cols = pieces[0].shape[1]
    for i, piece in enumerate(pieces):
        out_ref[:, pl.ds(pl.multiple_of(table[i] * cols, cols), cols)] = piece[...]


def join(pieces, places, chunks):
    rows, cols = pieces[0].shape
    count, ranks = len(pieces), len(chunks)
    chunk = rows // ranks
    table = jnp.stack([jnp.asarray(v, jnp.int32) for v in list(places) + list(chunks)])
    piece = pl.BlockSpec((chunk, cols), lambda i, t: (t[count + i], 0))
    return pl.pallas_call(
        join_kernel,
        grid_spec=pltpu.PrefetchScalarGridSpec(
            num_scalar_prefetch=1,
            grid=(ranks,),
            in_specs=[piece] * count,
            out_specs=pl.BlockSpec((chunk, cols * count), lambda i, t: (i, 0)),
        ),
        out_shape=jax.ShapeDtypeStruct((rows, cols * count), pieces[0].dtype),
        cost_estimate=takes(5),
        compiler_params=pltpu.CompilerParams(vmem_limit_bytes=60 << 20),
        name="join",
    )(table, *pieces)


def pack_kernel(table, *refs):
    *ins, out_ref = refs
    at = 0
    for ref in ins:
        out_ref[:, at : at + ref.shape[1]] = ref[...]
        at += ref.shape[1]


def pack(weights, c, at, size, steps):
    rows = weights[0].shape[0]
    cols = weights[0].shape[1] // 2
    table = jnp.asarray(c, jnp.int32).reshape(1)
    spec = pl.BlockSpec((rows, size), lambda n, t: (0, t[0] * (cols // size) + at // size + n))
    return pl.pallas_call(
        pack_kernel,
        grid_spec=pltpu.PrefetchScalarGridSpec(
            num_scalar_prefetch=1,
            grid=(steps,),
            in_specs=[spec] * len(weights),
            out_specs=pl.BlockSpec((rows, size * len(weights)), lambda n, t: (0, n)),
        ),
        out_shape=jax.ShapeDtypeStruct((rows, size * len(weights) * steps), weights[0].dtype),
        cost_estimate=takes(2),
        compiler_params=pltpu.CompilerParams(vmem_limit_bytes=60 << 20),
        name="pack",
    )(table, *weights)


def allowed_keys(first_ref, step, block, span):
    keys = lax.broadcasted_iota(jnp.int32, (block, span), 1)
    rows = lax.broadcasted_iota(jnp.int32, (block, span), 0)
    skip = block + HALO - span
    first = first_ref[...] - (step * block + skip)
    return (keys >= first) & (keys <= rows + (HALO - skip))


def spans_of(first, block):
    steps = first.shape[0] // block
    lowest = jnp.min(first.reshape(steps, block), axis=1)
    own = jnp.arange(steps, dtype=jnp.int32) + HALO // block
    return own - lowest // block + 1


def by_span(need, block, body):
    for count in range(1, HALO // block + 2):
        pl.when(need == count)(functools.partial(body, count * block))


def attend_kernel(late, base, need, q_ref, k_ref, v_ref, *refs):
    if late:
        first_ref, o_ref, lse_ref = refs
    else:
        ke_ref, ve_ref, first_ref, _, _, o_ref, lse_ref, keys, values = refs
    step = pl.program_id(1) + base
    block = q_ref.shape[0]
    if late:
        keys, values = k_ref, v_ref
    else:

        @pl.when(pl.program_id(1) == 0)
        def _():
            keys[:HALO] = ke_ref[...]
            keys[HALO:] = k_ref[...]
            values[:HALO] = ve_ref[...]
            values[HALO:] = v_ref[...]

    def body(span):
        at = (step + 1) * block + (0 if late else HALO) - span
        window = pl.ds(pl.multiple_of(at, block), span)
        raw = dot_last(q_ref[...], keys[window, :]) * (HD**-0.5)
        raw = jnp.where(allowed_keys(first_ref, step, block, span), raw, NEG_FILL)
        top = jnp.max(raw, axis=-1, keepdims=True)
        expo = jnp.exp(raw - top)
        denom = jnp.sum(expo, axis=-1, keepdims=True)
        probs = (expo * (1.0 / denom)).astype(BF)
        o_ref[...] = dot_plain(probs, values[window, :]).astype(BF)
        lse_ref[...] = top + jnp.log(denom)

    by_span(need[step], block, body)


def attend(q, k, v, halo, first, done=None, block=256):
    rows, local = q.shape
    heads = local // HD
    late = halo is None
    base = HALO // block if late else 0
    steps = rows // block - base if late else HALO // block
    row = pl.BlockSpec((block, HD), lambda h, i, t: (base + i, h))
    column = pl.BlockSpec((rows, HD), lambda h, i, t: (0, h))
    bound = pl.BlockSpec((block, 1), lambda h, i, t: (base + i, 0))
    norm = pl.BlockSpec((None, block, 1), lambda h, i, t: (h, base + i, 0))
    if late:
        in_specs, operands, scratch, aliases = [row, column, column, bound], (q, k, v, first), [], {}
    else:
        edge = [pl.BlockSpec((HALO, HD), lambda h, i, t, at=at: (0, h + at)) for at in (0, heads)]
        whole = pl.BlockSpec(memory_space=pl.ANY)
        in_specs = [row, column, column] + edge + [bound, whole, whole]
        operands = (q, k, v, halo, halo, first) + tuple(done)
        scratch = [pltpu.VMEM((HALO + rows, HD), BF)] * 2
        aliases = {7: 0, 8: 1}
    return pl.pallas_call(
        functools.partial(attend_kernel, late, base),
        grid_spec=pltpu.PrefetchScalarGridSpec(
            num_scalar_prefetch=1,
            grid=(heads, steps),
            in_specs=in_specs,
            out_specs=[row, norm],
            scratch_shapes=scratch,
        ),
        out_shape=[
            jax.ShapeDtypeStruct((rows, local), BF),
            jax.ShapeDtypeStruct((heads, rows, 1), F32),
        ],
        input_output_aliases=aliases,
        cost_estimate=takes(10 if late else 20),
        compiler_params=pltpu.CompilerParams(vmem_limit_bytes=60 << 20),
        name="attend_late" if late else "attend_early",
    )(spans_of(first[:, 0], block), *operands)


def rotate_back(grad, cos, sin):
    return grad * cos - pltpu.roll(grad, HD // 2, 1) * sin


def attend_back_kernel(
    need, q_ref, k_ref, v_ref, ke_ref, ve_ref, first_ref, lse_ref, do_ref, cos_ref, sin_ref,
    dq_ref, dk_ref, dv_ref, e_ref, keys, values, dkeys, dvalues,
):
    step = pl.program_id(1)
    block = q_ref.shape[0]
    scale = HD**-0.5

    @pl.when(step == 0)
    def _():
        keys[:HALO] = ke_ref[...]
        keys[HALO:] = k_ref[...]
        values[:HALO] = ve_ref[...]
        values[HALO:] = v_ref[...]
        dkeys[...] = jnp.zeros_like(dkeys)
        dvalues[...] = jnp.zeros_like(dvalues)

    def body(span):
        window = pl.ds(pl.multiple_of((step + 1) * block + HALO - span, block), span)
        query, dout = q_ref[...], do_ref[...]
        raw = dot_last(query, keys[window, :]) * scale
        allowed = allowed_keys(first_ref, step, block, span)
        probs = jnp.where(allowed, jnp.exp(raw - lse_ref[...]), 0.0)
        dprob = dot_last(dout, values[window, :])
        delta = jnp.sum(probs * dprob, axis=-1, keepdims=True)
        dscore = (probs * (dprob - delta)).astype(BF)
        mine = pl.ds(pl.multiple_of(HALO + step * block, block), block)
        dquery = dot_plain(dscore, keys[window, :]) * scale
        dq_ref[...] = rotate_back(dquery, cos_ref[mine, :], sin_ref[mine, :]).astype(BF)
        dkeys[window, :] += dot_rows(dscore, query)
        dvalues[window, :] += dot_rows(probs.astype(BF), dout)

    by_span(need[step], block, body)

    @pl.when(step == pl.num_programs(1) - 1)
    def _():
        dkey = rotate_back(dkeys[...] * scale, cos_ref[...], sin_ref[...])
        e_ref[0] = dkey[:HALO].astype(BF)
        dk_ref[...] = dkey[HALO:]
        e_ref[1] = dvalues[:HALO].astype(BF)
        dv_ref[...] = dvalues[HALO:]


def attend_back(q, k, v, halo, first, lse, dout, cos_tab, sin_tab, block=256):
    rows, local = q.shape
    heads = local // HD
    span = block + HALO
    column = pl.BlockSpec((rows, HD), lambda h, i, t: (0, h))
    piece = pl.BlockSpec((block, HD), lambda h, i, t: (i, h))
    table = pl.BlockSpec((HALO + rows, HD), lambda h, i, t: (0, 0))
    edge = pl.BlockSpec((HALO, HD), lambda h, i, t: (0, h))
    return pl.pallas_call(
        attend_back_kernel,
        grid_spec=pltpu.PrefetchScalarGridSpec(
            num_scalar_prefetch=1,
            grid=(heads, rows // block),
            in_specs=[
                piece,
                column,
                column,
                edge,
                pl.BlockSpec((HALO, HD), lambda h, i, t: (0, h + heads)),
                pl.BlockSpec((block, 1), lambda h, i, t: (i, 0)),
                pl.BlockSpec((None, block, 1), lambda h, i, t: (h, i, 0)),
                piece,
                table,
                table,
            ],
            out_specs=[
                piece,
                column,
                column,
                pl.BlockSpec((2, HALO, HD), lambda h, i, t: (0, 0, (h + heads // 2) % heads)),
            ],
            scratch_shapes=[pltpu.VMEM((HALO + rows, HD), BF)] * 2
            + [pltpu.VMEM((HALO + rows, HD), F32)] * 2,
        ),
        out_shape=[
            jax.ShapeDtypeStruct((rows, local), BF),
            jax.ShapeDtypeStruct((rows, local), F32),
            jax.ShapeDtypeStruct((rows, local), F32),
            jax.ShapeDtypeStruct((2, HALO, local), BF),
        ],
        cost_estimate=takes(43),
        compiler_params=pltpu.CompilerParams(vmem_limit_bytes=60 << 20),
        name="attend_back",
    )(spans_of(first[:, 0], block), q, k, v, halo, halo, first, lse, dout, cos_tab, sin_tab)


def ffn_kernel(first_half, seeded, shared_count, steps, table, h_ref, g_ref, own_ref, oth_ref, *refs):
    count = 2 if not first_half else int(seeded)
    starts, refs = refs[:count], refs[count + shared_count :]
    back_ref, act_own, act_oth, d_own, d_oth, *refs = refs
    if first_half:
        forth_ref, keep_ref = refs
        back, forth = back_ref, forth_ref
    else:
        *outs, back, forth = refs
    step = pl.program_id(0)
    hidden, grad = h_ref[...], g_ref[...]
    size = own_ref.shape[1] // 3

    if first_half:

        @pl.when(step == 0)
        def _():
            keep_ref[...] = hidden

    for w_ref, act_ref, d_ref in ((own_ref, act_own, d_own), (oth_ref, act_oth, d_oth)):
        both = dot_plain(hidden, w_ref[:, : 2 * size])
        dact = dot_plain(grad, w_ref[:, 2 * size :]).astype(BF).astype(F32)
        gate, up = both[:, :size], both[:, size:]
        sig = jax.nn.sigmoid(gate)
        silu = gate * sig
        act_ref[...] = (silu * up).astype(BF)
        d_ref[:, :size] = (dact * up * sig * (1.0 + gate * (1.0 - sig))).astype(BF)
        d_ref[:, size:] = (dact * silu).astype(BF)

    def add(first, last):
        tile = back_ref.shape[1] // 4
        for at in range(0, 4 * tile, tile):
            cols = slice(at, at + tile)
            more = dot_last(act_own[...], own_ref[cols, 2 * size :])
            more += dot_last(act_oth[...], oth_ref[cols, 2 * size :])
            grad = dot_last(d_own[...], own_ref[cols, : 2 * size])
            grad += dot_last(d_oth[...], oth_ref[cols, : 2 * size])
            if not first:
                more += forth[:, cols]
                grad += back[:, cols]
            elif not first_half:
                more += starts[1][:, cols]
                grad += starts[0][:, cols]
            elif seeded:
                more += starts[0][:, cols]
            if first_half or not last:
                forth[:, cols] = more
                back[:, cols] = grad
                continue
            back_ref[:, cols] = grad.astype(back_ref.dtype)
            if steps == 1 or len(outs) != 4:
                forth[:, cols] = more
                continue
            for i, out_ref in enumerate(outs):

                @pl.when(table[1 + i] == at // tile)
                def _():
                    out_ref[...] = more.astype(BF)

        if last and not first_half and (steps == 1 or len(outs) != 4):
            for i, out_ref in enumerate(outs):
                cols = out_ref.shape[1]
                at = pl.multiple_of(table[1 + i] * cols, cols)
                out_ref[...] = forth[:, pl.ds(at, cols)].astype(BF)

    if steps == 1:
        add(True, True)
    else:
        pl.when(step == 0)(lambda: add(True, False))
        if steps > 2:
            pl.when((step > 0) & (step < steps - 1))(lambda: add(False, False))
        pl.when(step == steps - 1)(lambda: add(False, True))


def feed_forward(j, place, places, hidden, grad_rows, w_own, w_oth, half, size, starts, shared, kind):
    chunk, width = hidden.shape
    rows = grad_rows.shape[0]
    first_half = places is None
    steps = half // size
    fixed = pl.BlockSpec((chunk, width), lambda n, t: (0, 0))
    at_j = pl.BlockSpec((chunk, width), lambda n, t: (j, 0))
    weight = pl.BlockSpec((width, 3 * size), lambda n, t: (0, n))
    table = jnp.stack([jnp.asarray(p, jnp.int32) for p in [place] + list(places or [])])
    starts = [] if starts is None else list(starts)
    operands = [hidden, grad_rows, w_own, w_oth] + starts
    in_specs = [fixed, at_j, weight, weight] + [fixed] * len(starts)
    act = pl.BlockSpec((chunk, size), lambda n, t: (j, n))
    both = pl.BlockSpec((chunk, 2 * size), lambda n, t: (j, n))
    out_specs = [fixed, act, act, both, both]
    out_shape = (
        [jax.ShapeDtypeStruct((chunk, width), kind)]
        + [jax.ShapeDtypeStruct((rows, half), BF)] * 2
        + [jax.ShapeDtypeStruct((rows, 2 * half), BF)] * 2
    )
    shared_at = [1, 2, 3, 4]
    if first_half:
        out_specs += [fixed, at_j]
        out_shape += [
            jax.ShapeDtypeStruct((chunk, width), F32),
            jax.ShapeDtypeStruct((rows, width), BF),
        ]
        shared_at.append(6)
    else:
        cols = width // len(places)
        out_specs += [pl.BlockSpec((chunk, cols), lambda n, t: (t[0], 0))] * len(places)
        out_shape += [jax.ShapeDtypeStruct((rows, cols), BF)] * len(places)
        shared_at += [5 + i for i in range(len(places))]
    aliases = {}
    if shared is not None:
        aliases = {1 + len(operands) + i: at for i, at in enumerate(shared_at)}
        in_specs += [pl.BlockSpec(memory_space=pl.ANY)] * len(shared)
        operands += list(shared)
    out = pl.pallas_call(
        functools.partial(
            ffn_kernel, first_half, len(starts) == 1, 0 if shared is None else len(shared), steps
        ),
        grid_spec=pltpu.PrefetchScalarGridSpec(
            num_scalar_prefetch=1,
            grid=(steps,),
            in_specs=in_specs,
            out_specs=out_specs,
            scratch_shapes=[] if first_half else [pltpu.VMEM((chunk, width), F32)] * 2,
        ),
        out_shape=out_shape,
        input_output_aliases=aliases,
        cost_estimate=takes(20),
        compiler_params=pltpu.CompilerParams(vmem_limit_bytes=60 << 20),
        name="feed_forward",
    )(table, *operands)
    sums = [out[0], out[5]] if first_half else out[0]
    return sums, [out[at] for at in shared_at]


def finish_kernel(dq, dk, dv, e_ref, d_own, d_oth, edges):
    step = pl.program_id(0)
    chunk, local = dq.shape
    lead = edges.shape[1] - e_ref.shape[1]

    @pl.when(step == 0)
    def _():
        edges[:, :lead] = jnp.zeros((2, lead, local), BF)
        edges[:, lead:] = e_ref[...]

    rows = pl.ds(pl.multiple_of(step * chunk, chunk), chunk)
    dkey = (dk[...] + edges[0, rows, :].astype(F32)).astype(BF)
    dvalue = (dv[...] + edges[1, rows, :].astype(F32)).astype(BF)
    cols = local // 2
    for ref, at in ((d_own, 0), (d_oth, cols)):
        ref[:, :cols] = dq[:, at : at + cols]
        ref[:, cols : 2 * cols] = dkey[:, at : at + cols]
        ref[:, 2 * cols :] = dvalue[:, at : at + cols]


def finish_attention(dq, dk, dv, edges, block=256):
    rows, local = dq.shape
    inner = 3 * local // 2
    row = lambda i: (i, 0)
    part = pl.BlockSpec((block, local), row)
    return pl.pallas_call(
        finish_kernel,
        grid=(rows // block,),
        in_specs=[part, part, part, pl.BlockSpec(edges.shape, lambda i: (0, 0, 0))],
        out_specs=[pl.BlockSpec((block, inner), row)] * 2,
        out_shape=[jax.ShapeDtypeStruct((rows, inner), BF)] * 2,
        scratch_shapes=[pltpu.VMEM((2, rows, local), BF)],
        cost_estimate=takes(4),
        compiler_params=pltpu.CompilerParams(vmem_limit_bytes=60 << 20),
        name="finish_attention",
    )(dq, dk, dv, edges)


def input_kernel(table, d_own, d_oth, w_own, w_oth, x_ref, dx_ref, *outs):
    step = pl.program_id(0)
    grad = dot_last(d_own[...], w_own[...]) + dot_last(d_oth[...], w_oth[...])
    normed, inv_dev = normalize(x_ref[...].astype(F32))
    grad = norm_back(grad, normed, inv_dev)
    keep = jnp.where(step == table[0], 1.0, 0.0)
    grad = (grad + keep * dx_ref[...]).astype(BF)
    for i, out_ref in enumerate(outs):
        width = out_ref.shape[1]
        for t in range(len(outs)):

            @pl.when(table[1 + i] == t)
            def _():
                out_ref[...] = grad[:, t * width : (t + 1) * width]


def input_parts(rank, places, d_own, d_oth, w_own, w_oth, full_x, dx1):
    rows, width = full_x.shape
    chunk = dx1.shape[0]
    inner = w_own.shape[1]
    cols = width // len(places)
    row = lambda i, t: (i, 0)
    once = lambda i, t: (0, 0)
    return pl.pallas_call(
        input_kernel,
        grid_spec=pltpu.PrefetchScalarGridSpec(
            num_scalar_prefetch=1,
            grid=(rows // chunk,),
            in_specs=[
                pl.BlockSpec((chunk, inner), row),
                pl.BlockSpec((chunk, inner), row),
                pl.BlockSpec((width, inner), once),
                pl.BlockSpec((width, inner), once),
                pl.BlockSpec((chunk, width), row),
                pl.BlockSpec((chunk, width), once),
            ],
            out_specs=[pl.BlockSpec((chunk, cols), row)] * len(places),
        ),
        out_shape=[jax.ShapeDtypeStruct((rows, cols), BF)] * len(places),
        cost_estimate=takes(20),
        compiler_params=pltpu.CompilerParams(vmem_limit_bytes=60 << 20),
        name="input_parts",
    )(
        jnp.stack([jnp.asarray(p, jnp.int32) for p in [rank] + list(places)]),
        d_own, d_oth, w_own, w_oth, full_x, dx1,
    )


def shares_kernel(table, m_ref, w_own, w_oth, keep_ref, mine_ref, *refs):
    cols = w_own.shape[1]
    keep_ref[...] = m_ref[...]
    out = dot_last(m_ref[:, :cols], w_own[...]) + dot_last(m_ref[:, cols:], w_oth[...])
    for j, ref in enumerate((mine_ref,) + refs):

        @pl.when(pl.program_id(0) == j)
        def _():
            ref[...] = out.astype(ref.dtype)


def output_shares(mixed, w_own, w_oth, turned):
    rows, local = mixed.shape
    width, cols = w_own.shape
    ranks = len(turned)
    chunk = rows // ranks
    once = lambda j, t: (0, 0)
    return pl.pallas_call(
        shares_kernel,
        grid_spec=pltpu.PrefetchScalarGridSpec(
            num_scalar_prefetch=1,
            grid=(ranks,),
            in_specs=[
                pl.BlockSpec((chunk, local), lambda j, t: (t[j], 0)),
                pl.BlockSpec((width, cols), once),
                pl.BlockSpec((width, cols), once),
            ],
            out_specs=[pl.BlockSpec((chunk, local), lambda j, t: (j, 0))]
            + [pl.BlockSpec((chunk, width), once)] * ranks,
        ),
        out_shape=[
            jax.ShapeDtypeStruct((rows, local), BF),
            jax.ShapeDtypeStruct((chunk, width), F32),
        ]
        + [jax.ShapeDtypeStruct((chunk, width), BF)] * (ranks - 1),
        cost_estimate=takes(7),
        compiler_params=pltpu.CompilerParams(vmem_limit_bytes=60 << 20),
        name="output_shares",
    )(jnp.stack(turned).astype(jnp.int32), mixed, w_own, w_oth)


def dmixed_kernel(table, *refs):
    *chunks, w_own, w_oth, keep_ref, d_ref = refs
    cols = w_own.shape[1]
    for j in range(len(chunks)):

        @pl.when(pl.program_id(0) == j)
        def _():
            chunk = chunks[j][...]
            keep_ref[...] = chunk
            d_ref[:, :cols] = dot_plain(chunk, w_own[...]).astype(BF)
            d_ref[:, cols:] = dot_plain(chunk, w_oth[...]).astype(BF)


def dmixed(chunks, w_own, w_oth, turned):
    chunk, width = chunks[0].shape
    cols = w_own.shape[1]
    ranks = len(chunks)
    once = lambda j, t: (0, 0)
    return pl.pallas_call(
        dmixed_kernel,
        grid_spec=pltpu.PrefetchScalarGridSpec(
            num_scalar_prefetch=1,
            grid=(ranks,),
            in_specs=[pl.BlockSpec((chunk, width), once)] * ranks
            + [pl.BlockSpec((width, cols), once)] * 2,
            out_specs=[
                pl.BlockSpec((chunk, width), lambda j, t: (j, 0)),
                pl.BlockSpec((chunk, 2 * cols), lambda j, t: (t[j], 0)),
            ],
        ),
        out_shape=[
            jax.ShapeDtypeStruct((chunk * ranks, width), BF),
            jax.ShapeDtypeStruct((chunk * ranks, 2 * cols), BF),
        ],
        cost_estimate=takes(7),
        compiler_params=pltpu.CompilerParams(vmem_limit_bytes=60 << 20),
        name="dmixed",
    )(jnp.stack(turned).astype(jnp.int32), *chunks, w_own, w_oth)


def norm_kernel(table, x_ref, mine_ref, *refs):
    *others, resid_ref, h_ref = refs
    total = x_ref[...].astype(F32) + mine_ref[...]
    for ref in others:
        total = total + ref[...].astype(F32)
    resid_ref[...] = total
    h_ref[...] = normalize(total)[0].astype(BF)


def norm_chunk(rank, full_x, mine, others):
    chunk, width = mine.shape
    block = chunk // 3
    row = pl.BlockSpec((block, width), lambda i, t: (i, 0))
    return pl.pallas_call(
        norm_kernel,
        grid_spec=pltpu.PrefetchScalarGridSpec(
            num_scalar_prefetch=1,
            grid=(3,),
            in_specs=[pl.BlockSpec((block, width), lambda i, t: (t[0] * 3 + i, 0)), row]
            + [row] * len(others),
            out_specs=[row, row],
        ),
        out_shape=[
            jax.ShapeDtypeStruct((chunk, width), F32),
            jax.ShapeDtypeStruct((chunk, width), BF),
        ],
        cost_estimate=takes(4),
        compiler_params=pltpu.CompilerParams(vmem_limit_bytes=60 << 20),
        name="norm_chunk",
    )(jnp.asarray(rank, jnp.int32).reshape(1), full_x, mine, *others)


def back_kernel(g_ref, resid_ref, mine_ref, *refs):
    *others, dx_ref, da_ref = refs
    total = mine_ref[...]
    for ref in others:
        total = total + ref[...].astype(F32)
    normed, inv_dev = normalize(resid_ref[...])
    dx = g_ref[...].astype(F32) + norm_back(total, normed, inv_dev)
    dx_ref[...] = dx
    da_ref[...] = dx.astype(BF)


def back_chunk(grad_rows, resid1, mine, others):
    chunk, width = mine.shape
    block = chunk // 3
    row = pl.BlockSpec((block, width), lambda i: (i, 0))
    return pl.pallas_call(
        back_kernel,
        grid=(3,),
        in_specs=[row] * (3 + len(others)),
        out_specs=[row, row],
        out_shape=[
            jax.ShapeDtypeStruct((chunk, width), F32),
            jax.ShapeDtypeStruct((chunk, width), BF),
        ],
        cost_estimate=takes(4),
        compiler_params=pltpu.CompilerParams(vmem_limit_bytes=60 << 20),
        name="back_chunk",
    )(grad_rows, resid1, mine, *others)


def grads_kernel(count, *refs):
    *ins, out_ref = refs
    at = 0
    for left, right in zip(ins[:count], ins[count : 2 * count]):
        cols = right.shape[1]
        total = dot_rows(left[...], right[...])
        if len(ins) > 2 * count:
            total = total + ins[-1][:, at : at + cols].astype(F32)
        out_ref[:, at : at + cols] = total.astype(BF)
        at += cols


def grads(lefts, rights, other=None):
    rows, width = lefts[0].shape
    cols = sum(r.shape[1] for r in rights)
    block = 512
    in_specs = [pl.BlockSpec((rows, block), lambda m: (0, m))] * len(lefts)
    in_specs += [pl.BlockSpec(r.shape, lambda m: (0, 0)) for r in rights]
    out = pl.BlockSpec((block, cols), lambda m: (m, 0))
    operands = list(lefts) + list(rights)
    if other is not None:
        in_specs.append(out)
        operands.append(other)
    return pl.pallas_call(
        functools.partial(grads_kernel, len(lefts)),
        grid=(width // block,),
        in_specs=in_specs,
        out_specs=out,
        out_shape=jax.ShapeDtypeStruct((width, cols), BF),
        cost_estimate=takes(10),
        compiler_params=pltpu.CompilerParams(vmem_limit_bytes=60 << 20),
        name="grads",
    )(*operands)


def after(value, *others):
    return lax.optimization_barrier((value,) + others)[0]


class Plane:
    def __init__(self):
        self.nc, self.nt = lax.axis_size("ctx"), lax.axis_size("tp")
        assert self.nc == 2 and self.nt % 2 == 0
        self.hi = self.nt // self.nc
        self.ranks = self.nc * self.hi
        tp_place = lax.axis_index("tp")
        self.c = lax.axis_index("ctx")
        self.h, self.k = tp_place // self.nc, tp_place % self.nc
        self.r = self.c * self.hi + self.h

    def perm(self, move):
        pairs = []
        for c in range(self.nc):
            for h in range(self.hi):
                for k in range(self.nc):
                    c2, h2, k2 = move(c, h, k)
                    pairs.append((c * self.nt + h * self.nc + k, c2 * self.nt + h2 * self.nc + k2))
        return pairs

    def spread_rows(self, block):
        got = []
        for jh in range(self.hi):
            for jk in range(self.nc):
                move = lambda c, h, k: (k ^ jk, h ^ jh, c)
                place = (self.h ^ jh) * self.nc + (self.c ^ jk)
                got.append((place, lax.ppermute(block, PLANE, self.perm(move))))
        return got

    def spread_own(self, block, jh=0):
        got = []
        for jk in range(self.nc):
            move = lambda c, h, k: (k ^ jk, h, c)
            place = (self.h ^ jh) * self.nc + (self.c ^ jk)
            got.append((place, lax.ppermute(block, PLANE, self.perm(move))))
        return got

    def turn_pairs(self, block, jh):
        return lax.ppermute(block, PLANE, self.perm(lambda c, h, k: (c, h ^ jh, k)))

    def block_places(self):
        return [
            (self.h ^ jh) * self.nc + (self.c ^ jk) for jh in range(self.hi) for jk in range(self.nc)
        ]

    def collect_blocks(self, pieces):
        moves = [
            lambda c, h, k, jh=jh, jk=jk: (k, h ^ jh, c ^ jk)
            for jh in range(self.hi)
            for jk in range(self.nc)
        ]
        return [lax.ppermute(p, PLANE, self.perm(m)) for p, m in zip(pieces, moves)]

    def sum_pairs(self, pieces):
        sent = [
            lax.ppermute(
                pieces[jh * self.nc + jk],
                PLANE,
                self.perm(lambda c, h, k, jh=jh: (c, h ^ jh, k)),
            )
            for jh in range(1, self.hi)
            for jk in range(self.nc)
        ]
        return [sent[jk :: self.nc] for jk in range(self.nc)]

    def sum_blocks(self, own):
        return [
            lax.ppermute(own[jk], PLANE, self.perm(lambda c, h, k, jk=jk: (k, h, c ^ jk)))
            for jk in range(self.nc)
        ]

    def swap(self, value, j):
        def move(c, h, k):
            rank = (c * self.hi + h) ^ j
            return rank // self.hi, rank % self.hi, k

        return lax.ppermute(value, PLANE, self.perm(move))

    def chunk_of(self, value, j):
        size = value.shape[0] // self.ranks
        return lax.dynamic_slice_in_dim(value, (self.r ^ j) * size, size, 0)

    def turn(self, value):
        return jnp.concatenate([self.chunk_of(value, j) for j in range(self.ranks)], axis=0)

    def gather(self, mine, use=None):
        use = use or (lambda j, chunk: chunk[:8, :128])
        out = [mine]
        if self.ranks != 4:
            out += [self.swap(mine, j) for j in range(1, self.ranks)]
            for j in range(self.ranks):
                use(j, out[j])
            return out
        near, far = self.swap(mine, 1), self.swap(mine, 2)
        near, far, _ = lax.optimization_barrier((near, far, use(0, mine)))
        half = mine.shape[0] // 2
        corner = [self.swap(near[:half], 2), self.swap(far[half:], 1)]
        use(1, near)
        last = use(2, far)
        corner = jnp.concatenate(lax.optimization_barrier((*corner, last))[:2], axis=0)
        use(3, corner)
        return [mine, near, far, corner]

    def pair(self, value):
        perm = [(t, t ^ 1) for t in range(self.nt)]
        return lax.ppermute(value, "tp", perm)


def body(
    tokens, cotangent, lengths, order, w_query, w_key, w_value, w_output, w_gate, w_up, w_down
):
    plane = Plane()
    rows = tokens.shape[0]
    nf, nc, nt, ranks = lax.axis_size("fsdp"), plane.nc, plane.nt, plane.ranks
    z = lax.axis_index("fsdp")
    chunk = rows // ranks
    head_cols = w_query.shape[1] // nc
    heads = head_cols // HD
    hidden_cols = w_gate.shape[1] // nc
    half = hidden_cols // 2
    size = min(256, half)

    def over_fsdp(shard):
        return lax.all_gather(shard, "fsdp", axis=0, tiled=True)

    fence = lambda *values: lax.optimization_barrier(values)
    turned = [plane.r ^ j for j in range(ranks)]

    qkv_own = over_fsdp(pack((w_query, w_key, w_value), plane.c, 0, head_cols, 1))
    places, got_x = zip(*plane.spread_rows(tokens))
    base = (z * nc + plane.k) * rows - HALO
    index = base + jnp.arange(HALO + rows, dtype=jnp.int32)
    starts = first_of(index, slots(lengths, order))
    within = index - starts
    first = (starts[HALO:] - base)[:, None]
    lane = jnp.arange(HD, dtype=jnp.int32)
    freq = jnp.exp((lane % (HD // 2)).astype(F32) * (-2.0 * math.log(10000.0) / HD))
    angle = within.astype(F32)[:, None] * freq[None, :]
    cos_tab = jnp.cos(angle)
    sin_tab = jnp.sin(angle) * jnp.where(lane < HD // 2, -1.0, 1.0)[None, :]
    qkv_own, cos_tab, sin_tab, first, *got_x = fence(qkv_own, cos_tab, sin_tab, first, *got_x)
    qkv_oth = plane.pair(qkv_own)
    w_output, cotangent = fence(w_output, cotangent, *got_x)[:2]
    wo_own = over_fsdp(pack((w_output,), plane.c, 0, head_cols, 1))
    own_g = plane.spread_own(cotangent)
    far_g = [plane.turn_pairs(cotangent, jh) for jh in range(1, plane.hi)]
    places_g = [place for place, _ in own_g]

    full_x, hidden1, query, key, value, edge = project(
        got_x, places, qkv_own, qkv_oth, cos_tab, sin_tab, heads
    )
    onward = []
    for f in range(nf):
        for h in range(plane.hi):
            for k in range(nc):
                to = f * nc + k + 1
                if to < nf * nc:
                    onward.append((f * nt + h * nc + k, to // nc * nt + h * nc + to % nc))
    backward = [(b, a) for a, b in onward]
    halo = lax.ppermute(edge, ("fsdp", "tp"), onward)
    wo_oth = plane.pair(after(wo_own, edge))
    late = attend(query, key, value, None, first)
    late, far_g, own_g = fence(late, far_g, [piece for _, piece in own_g])
    got_g = []
    for jh in range(1, plane.hi):
        for place, piece in plane.spread_own(far_g[jh - 1], jh):
            places_g.append(place)
            got_g.append(piece)
    halo, wo_own, wo_oth, *late = fence(halo, wo_own, wo_oth, *late)
    shard0 = pack(after((w_gate, w_up, w_down), halo), plane.c, 0, size, half // size)
    own0 = over_fsdp(shard0)
    mixed, lse = attend(query, key, value, after(halo, shard0), first, late)
    early = len(got_g) // 2
    mixed, got_g[:early] = fence(mixed, got_g[:early])

    mixed_rows, mine, *shares = output_shares(mixed, wo_own, wo_oth, turned)
    sent = [plane.swap(shares[j - 1], j) for j in range(ranks - 1, 0, -1)]
    mine, *got_g = fence(mine, *own_g, *got_g)
    grad_rows = join(got_g, places_g, turned)
    shard1 = pack(after((w_gate, w_up, w_down), mine), plane.c, half, size, half // size)
    own1 = over_fsdp(shard1)
    mine, grad_rows, *sent = fence(mine, grad_rows, *sent, shard1)[:-1]
    oth0 = plane.pair(after(own0, sent[0]))
    resid1, mine = norm_chunk(plane.r, full_x, mine, sent)

    sums, shared = {}, None

    def first_half(j, piece):
        nonlocal shared
        sums[j], shared = feed_forward(
            j, turned[j], None, piece, grad_rows, own0, oth0, half, size,
            None if j else [resid1], shared, F32,
        )
        return sums[j][0]

    pieces = plane.gather(mine, first_half)
    act_own, act_oth, d_own, d_oth, hidden2 = shared

    def halves(lefts, rights_own, rights_oth):
        return grads(lefts, rights_own, plane.pair(grads(lefts, rights_oth)))

    def reduce_rows(total):
        return lax.psum_scatter(total, "fsdp", scatter_dimension=0, tiled=True)

    def exchange(mine):
        return lax.ppermute(mine, "ctx", [(0, 1), (1, 0)])

    def both_parts(mine, other):
        here = plane.c == 0
        return jnp.where(here, mine, other), jnp.where(here, other, mine)

    lefts = (grad_rows, hidden2)
    rights0, other0 = (act_own, d_own), grads(lefts, (act_oth, d_oth))

    oth1 = plane.pair(after(own1, act_own))
    other0, oth1 = fence(other0, oth1)
    other0 = plane.pair(other0)
    totals, sent, shared = {}, [], None
    for at, j in enumerate(list(range(ranks - 1, 0, -1)) + [0]):
        piece = pieces[j]
        if at == 1:
            rights0 = after(rights0, totals[ranks - 1])
            total0 = grads(lefts, rights0, other0)
            share0 = reduce_rows(total0)
            piece = after(piece, total0)
        if at > 2:
            piece, sent[at - 3] = fence(piece, sent[at - 3])
        totals[j], shared = feed_forward(
            j, turned[j], plane.block_places(), piece, grad_rows, own1, oth1, half, size,
            sums[j], shared, BF if j else F32,
        )
        if j:
            sent.append(plane.swap(totals[j], j))
    act_own, act_oth, d_own, d_oth, *forth = shared
    act_oth, *sent[:-1] = fence(act_oth, *sent[:-1])
    other1 = grads(lefts, (act_oth, d_oth))
    mine, sent[-1], other1 = fence(totals[0], sent[-1], other1)
    other1 = plane.pair(other1)
    dx1, da = back_chunk(grad_rows, resid1, mine, sent)

    def own_grads(j, _):
        nonlocal total1
        if total1 is None:
            total1 = grads(lefts, fence(act_own, d_own, da)[:2], other1)
        return total1

    total1 = None
    da_pieces = plane.gather(da, own_grads)
    share1 = reduce_rows(fence(total1, *da_pieces[1:3])[0])

    da, dout = dmixed(da_pieces, wo_own, wo_oth, turned)
    dout, share0, *forth = fence(dout, share0, *forth)
    others = [exchange(share0)]
    pairs = plane.sum_pairs(forth)
    dquery, dkey, dvalue, edges = attend_back(
        query, key, value, halo, first, lse, dout, cos_tab, sin_tab
    )
    edges = lax.ppermute(edges, ("fsdp", "tp"), backward)
    dquery, pairs, others[0] = fence(dquery, pairs, others[0])
    own = [
        functools.reduce(jnp.add, [p.astype(F32) for p in [forth[jk]] + pairs[jk]]).astype(BF)
        for jk in range(nc)
    ]
    forth = plane.sum_blocks(own)
    da, mixed_rows = fence(da, mixed_rows, *own)[:2]
    total_out = halves((da,), (mixed_rows[:, :head_cols],), (mixed_rows[:, head_cols:],))
    share_out = reduce_rows(total_out)
    edges = after(edges, total_out)
    others.append(exchange(after(share1, *forth)))
    d_own, d_oth = finish_attention(dquery, dkey, dvalue, edges)
    other2 = grads((hidden1,), (d_oth,))
    other2, *forth = fence(other2, *forth)
    other2 = plane.pair(other2)
    layer_out = functools.reduce(jnp.add, [p.astype(F32) for p in forth]).astype(BF)
    other2, layer_out = fence(other2, layer_out)
    total2 = grads((hidden1,), (d_own,), other2)
    share2 = reduce_rows(total2)
    d_own, d_oth = fence(d_own, d_oth, total2)[:2]
    parts = input_parts(
        plane.r, plane.block_places(), d_own, d_oth, qkv_own, qkv_oth, full_x, dx1
    )
    *parts, others[1] = fence(*parts, others[1])
    back = plane.collect_blocks(parts)

    done = [both_parts(share0, others[0]), both_parts(share1, others[1])]
    grad_down = jnp.concatenate([done[s][c][:, :half] for c in range(2) for s in range(2)], axis=1)
    grad_gate, grad_up = (
        jnp.concatenate(
            [
                done[s][c][:, half + (2 * n + which) * size : half + (2 * n + which + 1) * size]
                for c in range(2)
                for s in range(2)
                for n in range(half // size)
            ],
            axis=1,
        )
        for which in range(2)
    )
    other2 = exchange(share2)
    back, other2, share2 = fence(back, other2, share2)
    last = both_parts(share2, other2)
    grad_query, grad_key, grad_value = (
        jnp.concatenate([p[:, i * head_cols : (i + 1) * head_cols] for p in last], axis=1)
        for i in range(3)
    )
    grad_output = jnp.concatenate(
        both_parts(share_out, exchange(after(share_out, back[0]))), axis=1
    )
    input_grad = functools.reduce(jnp.add, [p.astype(F32) for p in back]).astype(BF)
    grads_out = (grad_query, grad_key, grad_value, grad_output, grad_gate, grad_up, grad_down)
    return (layer_out, input_grad) + tuple(g.astype(F32) for g in grads_out)


def solution(mesh):
    rows = P(("fsdp", "ctx"), "tp")
    weight = P("fsdp", "tp")
    return jax.shard_map(
        body,
        mesh=mesh,
        in_specs=(rows, rows, P(), P()) + (weight,) * 7,
        out_specs=(rows, rows) + (weight,) * 7,
        check_vma=False,
    )
```
